256 devices in a mesh: slab: 32 (over y, z), chan: 8 (over x, core).
Axes of the slice: x: 4, y: 4, z: 8, core: 2. Of those that a mesh axis runs over, the one named last changes fastest.
Arguments:
- state_field: bfloat16 [2, 16, 256, 256, 256], P(None, 'chan', 'slab'), may hold values from -6 to 6
- spectral_weights: bfloat16 [16, 16, 64, 32, 2, 64], P(None, None, 'chan', None, None, 'slab'), may hold values from -1 to 1
- channel_shift: bfloat16 [16], P('chan'), may hold values from -3 to 3
Outputs:
- layer_output: bfloat16 [2, 16, 256, 256, 256], P(None, 'chan', 'slab')
The draws below stay inside these ranges and needn't reach their ends.
All inputs are finite; a program needn't handle non-finite values.
Results may differ from the reference program's by a relative error of at most 0.015.
Values may be sent and summed in bfloat16 or wider, within the bound.
A program may use at most 64 MiB of HBM per device.

```python
import jax
import jax.numpy as jnp
from jax import lax

NG = 256
CH = 16
KM = 32
SAMPLES = 2


def shard_levels(key, dims, pieces, low, top_value):
    factor_of = 1.0
    for axis_at, blocks in pieces:
        draws = jax.random.uniform(jax.random.fold_in(jax.random.fold_in(key, 6), axis_at), (blocks,), jnp.float32, low / len(pieces), top_value / len(pieces))
        factor_of = factor_of * jnp.repeat(jnp.exp(draws), dims[axis_at] // blocks).reshape((-1,) + (1,) * (len(dims) - 1 - axis_at))
    return factor_of


def centred(own_key, extent, scale, reach, pieces=(), kind=jnp.bfloat16):
    factor_of = shard_levels(own_key, extent, pieces, -0.22, 0.18) if pieces else 1.0
    entries = jax.random.normal(own_key, extent, jnp.float32) * scale * factor_of
    return jnp.minimum(jnp.maximum(entries, -reach), reach).astype(kind)


def setup_inputs(seed: int = 0) -> dict:
    keys = jax.random.split(jax.random.key(seed), 4)
    state_field = centred(keys[0], (SAMPLES, CH, NG, NG, NG), 1.0, 6.0, ((1, 8), (2, 32)))
    spectral_weights = centred(keys[1], (CH, CH, 2 * KM, KM, 2, 2 * KM), (2 * CH) ** -0.5, 1.0, ((2, 8), (5, 32)))
    channel_shift = centred(keys[2], (CH,), 0.5, 3.0, ((0, 8),))
    return {"state_field": state_field, "spectral_weights": spectral_weights, "channel_shift": channel_shift}


def kept_freqs(mode_count, grid_side):
    index = jnp.arange(mode_count, dtype=jnp.int32)
    return jnp.where(index < mode_count // 2, index, index + grid_side - mode_count)

def angles(freq_list, grid_side):
    places = jnp.arange(grid_side, dtype=jnp.int32)
    product = freq_list[:, None] * places[None, :] % grid_side
    return product.astype(jnp.float32) * (2.0 * jnp.pi / grid_side)

def make_tables(grid_side, kept):
    bf = jnp.bfloat16
    fwd_scale = 1.0 / jnp.sqrt(jnp.float32(grid_side))
    inv_scale = 1.0 / jnp.sqrt(jnp.float32(2 * kept))
    z_freqs = jnp.arange(kept, dtype=jnp.int32)
    two_freqs = kept_freqs(2 * kept, grid_side)
    theta_z = angles(z_freqs, grid_side)
    theta_two = angles(two_freqs, grid_side)
    cos_z = jnp.cos(theta_z).T
    sin_z = jnp.sin(theta_z).T
    table_z = (jnp.stack([cos_z, -sin_z], -1) * fwd_scale).astype(bf)
    cos_t = jnp.cos(theta_two).T
    sin_t = jnp.sin(theta_two).T
    table_y = (jnp.stack([jnp.stack([cos_t, -sin_t], 1), jnp.stack([sin_t, cos_t], 1)], 0) * fwd_scale).astype(bf)
    table_x = (jnp.stack([jnp.stack([cos_t, -sin_t], -1), jnp.stack([sin_t, cos_t], -1)], 1) * fwd_scale).astype(bf)
    cos_m = jnp.cos(theta_two)
    sin_m = jnp.sin(theta_two)
    inv_x = (jnp.stack([jnp.stack([cos_m, sin_m], -1), jnp.stack([-sin_m, cos_m], -1)], 1) * inv_scale).astype(bf)
    inv_y = (jnp.stack([jnp.stack([cos_m, sin_m], 1), jnp.stack([-sin_m, cos_m], 1)], 0) * inv_scale).astype(bf)
    weight_k = jnp.where(z_freqs == 0, 1.0, 2.0).astype(jnp.float32)[:, None]
    inv_z = (jnp.stack([weight_k * jnp.cos(theta_z), -weight_k * jnp.sin(theta_z)], 1) * inv_scale).astype(bf)
    return (table_z, table_y, table_x, inv_x, inv_y, inv_z)

def reference(state_field, spectral_weights, channel_shift):
    f32 = jnp.float32
    bf = jnp.bfloat16
    table_z, table_y, table_x, inv_x, inv_y, inv_z = make_tables(NG, KM)
    flat_grids = state_field.reshape(SAMPLES * CH, NG, NG, NG)

    def forward_one(one_grid):
        coef_z = jnp.einsum('xyz,zkp->xkpy', one_grid.astype(f32), table_z.astype(f32)).astype(bf)
        coef_y = jnp.einsum('xkpy,pyqn->xkqn', coef_z.astype(f32), table_y.astype(f32)).astype(bf)
        coef_x = jnp.einsum('xkpn,xpmq->mkqn', coef_y.astype(f32), table_x.astype(f32)).astype(bf)
        return coef_x
    spectra = lax.map(forward_one, flat_grids).reshape(SAMPLES, CH, 2 * KM, KM, 2, 2 * KM)
    spec_re = spectra[..., 0, :].astype(f32)
    spec_im = spectra[..., 1, :].astype(f32)
    wgt_re = spectral_weights[..., 0, :].astype(f32)
    wgt_im = spectral_weights[..., 1, :].astype(f32)
    mixed_re = jnp.einsum('bimkj,iomkj->bomkj', spec_re, wgt_re) - jnp.einsum('bimkj,iomkj->bomkj', spec_im, wgt_im)
    mixed_im = jnp.einsum('bimkj,iomkj->bomkj', spec_re, wgt_im) + jnp.einsum('bimkj,iomkj->bomkj', spec_im, wgt_re)
    mixed = jnp.stack([mixed_re, mixed_im], -2).astype(bf)
    flat_mixed = mixed.reshape(SAMPLES * CH, 2 * KM, KM, 2, 2 * KM)
    shifts = jnp.tile(channel_shift, SAMPLES)

    def inverse_one(packed):
        one_spec, shift_value = packed
        split_spec = one_spec.astype(f32)
        back_x = jnp.einsum('mkpn,mpxq->xkqn', split_spec, inv_x.astype(f32)).astype(bf)
        back_y = jnp.einsum('xkpn,pnqy->xkqy', back_x.astype(f32), inv_y.astype(f32)).astype(bf)
        summed = jnp.einsum('xkpy,kpz->xyz', back_y.astype(f32), inv_z.astype(f32))
        return jax.nn.gelu(summed + shift_value.astype(f32), approximate=False).astype(bf)
    result = lax.map(inverse_one, (flat_mixed, shifts))
    return result.reshape(SAMPLES, CH, NG, NG, NG)
```

```python
import jax
import jax.numpy as jnp
import ml_dtypes
import numpy as np
from jax import lax
from jax.experimental import pallas as pl
from jax.experimental.pallas import tpu as pltpu
from jax.sharding import PartitionSpec as P

NG = 256
KM = 32
NS = 32
NC = 8
XL = NG // NS
ML = 2 * KM // NC
F32 = jnp.float32
BF = jnp.bfloat16
MESH = pl.DeviceIdType.MESH


def make_tables():
    j = np.arange(NG)
    f2 = np.arange(2 * KM)
    f2 = np.where(f2 < KM, f2, f2 + NG - 2 * KM)
    unit = np.float32(2.0 * np.pi / NG)
    tz = ((np.arange(KM)[:, None] * j[None, :]) % NG).astype(np.float32) * unit
    t2 = ((f2[:, None] * j[None, :]) % NG).astype(np.float32) * unit
    cz, sz = np.cos(tz), np.sin(tz)
    c2, s2 = np.cos(t2), np.sin(t2)
    fwd, inv = 1.0 / 16.0, 1.0 / 8.0

    wz = np.zeros((2, 2, NG, 2, 2, 2, KM), np.float32)
    for b in range(2):
        for c in range(2):
            wz[b, c, :, 0, c, b, :] = cz.T * fwd
            wz[b, c, :, 1, c, b, :] = -sz.T * fwd
    wz = wz.reshape(4 * NG, 256)
    order = np.concatenate([np.arange(0, 2 * KM, 2), np.arange(1, 2 * KM, 2)])
    wy = np.concatenate([c2[order], s2[order]], 0) * fwd
    c8, s8 = c2.reshape(NC, ML, NG), s2.reshape(NC, ML, NG)
    wx = np.zeros((NC, 2, ML, NG, 2), np.float32)
    wx[:, 0, :, :, 0], wx[:, 0, :, :, 1] = c8, s8
    wx[:, 1, :, :, 0], wx[:, 1, :, :, 1] = -s8, c8
    wx = wx.reshape(2 * 2 * KM, 2 * NG) * fwd
    ix = np.zeros((NG, 2, NC, 2, ML), np.float32)
    ct, st = c8.transpose(2, 0, 1), s8.transpose(2, 0, 1)
    ix[:, 0, :, 0], ix[:, 0, :, 1] = ct, -st
    ix[:, 1, :, 0], ix[:, 1, :, 1] = st, ct
    ix = ix.reshape(2 * NG, 2 * 2 * KM) * inv
    iy = np.zeros((2, NG, 2, 2, KM), np.float32)
    for h in range(2):
        ch, sh = c2[h::2].T, s2[h::2].T
        iy[0, :, h, 0], iy[0, :, h, 1] = ch, -sh
        iy[1, :, h, 0], iy[1, :, h, 1] = sh, ch
    iy = iy.reshape(2 * NG, 4 * KM) * inv
    wk = np.where(np.arange(KM) == 0, 1.0, 2.0)[:, None]
    iz = np.zeros((2, 2, 2, 2, 2, KM, NG), np.float32)
    for b in range(2):
        for o in range(2):
            iz[b, o, 0, o, b] = wk * cz * inv
            iz[b, o, 1, o, b] = -wk * sz * inv
    iz = iz.reshape(4, 256, NG)
    ew = np.zeros((KM, 2, 2, 2, KM), np.float32)
    for h in range(2):
        for b in range(2):
            ew[:, h, h, b, :] = np.eye(KM)
    ew = ew.reshape(KM, 256)
    return tuple(np.asarray(t).astype(ml_dtypes.bfloat16) for t in (wz, wy, wx, ix, iy, iz, ew))


def forward_kernel(
    state, w2d, wz, wy, wx, ix, ew, out,
    xbuf, wraw, wzb, wyb, wxb, ixb, ewb, tmp, wtmp, wgt,
    send1, recv1, send2, recv2, send3, recv3, send4, recv4,
    in_sem, tab_sem, ssem, rsem,
):
    slab = lax.axis_index("slab")
    chan = lax.axis_index("chan")

    loads = []
    for at, (src, dst) in enumerate(
        ((wz, wzb), (wy, wyb), (w2d, wraw), (wx, wxb), (ix, ixb), (ew, ewb))
    ):
        loads.append(pltpu.make_async_copy(src, dst, tab_sem.at[at]))
    planes = [
        pltpu.make_async_copy(state.at[:, :, x], xbuf.at[x], in_sem.at[x]) for x in range(XL)
    ]
    loads[0].start()
    planes[0].start()
    loads[1].start()
    for x in range(1, XL):
        planes[x].start()
    for at in range(2, 6):
        loads[at].start()

    barrier = pltpu.get_barrier_semaphore()

    def greet_slab(j, carry):
        pl.semaphore_signal(
            barrier, inc=1, device_id=(lax.rem(slab + j, NS), chan), device_id_type=MESH
        )
        return carry

    def greet_chan(j, carry):
        pl.semaphore_signal(
            barrier, inc=1, device_id=(slab, lax.rem(chan + j, NC)), device_id_type=MESH
        )
        return carry

    lax.fori_loop(1, NS, greet_slab, 0)
    lax.fori_loop(1, NC, greet_chan, 0)

    loads[0].wait()
    loads[1].wait()
    for x in range(XL):
        planes[x].wait()
        four = jnp.concatenate([xbuf[x, b, c] for b in range(2) for c in range(2)], axis=1)
        coef_z = jnp.dot(four, wzb[...], preferred_element_type=F32).astype(BF)
        u = jnp.dot(wyb[...], coef_z, preferred_element_type=F32)
        re = u[:64, :128] + u[64:, 128:]
        im = u[:64, 128:] - u[64:, :128]
        for h in range(2):
            tmp[h, pl.ds(2 * x, NS, stride=16), :] = re[h * NS : (h + 1) * NS]
            tmp[h, pl.ds(2 * x + 1, NS, stride=16), :] = im[h * NS : (h + 1) * NS]
    for h in range(2):
        send1[:, :, h * 128 : (h + 1) * 128] = tmp[h].astype(BF).reshape(NS, 16, 128)

    pl.semaphore_wait(barrier, NS - 1 + NC - 1)

    def slab_exchange(send, recv, at):
        def post(j, carry):
            peer = lax.rem(slab + j, NS)
            pltpu.make_async_remote_copy(
                src_ref=send.at[peer],
                dst_ref=recv.at[slab],
                send_sem=ssem.at[at],
                recv_sem=rsem.at[at],
                device_id=(peer, chan),
                device_id_type=MESH,
            ).start()
            return carry

        lax.fori_loop(1, NS, post, 0)
        recv[slab] = send[slab]

    def chan_exchange(send, recv, at):
        def post(j, carry):
            peer = lax.rem(chan + j, NC)
            pltpu.make_async_remote_copy(
                src_ref=send.at[peer],
                dst_ref=recv.at[chan],
                send_sem=ssem.at[at],
                recv_sem=rsem.at[at],
                device_id=(slab, peer),
                device_id_type=MESH,
            ).start()
            return carry

        lax.fori_loop(1, NC, post, 0)
        recv[chan] = send[chan]

    def finish(send, recv, at, n):
        some = pl.ds(0, n - 1)
        pltpu.make_async_copy(recv.at[some], recv.at[some], rsem.at[at]).wait()

    def finish_send(send, at, n):
        some = pl.ds(0, n - 1)
        pltpu.make_async_copy(send.at[some], send.at[some], ssem.at[at]).wait()

    slab_exchange(send1, recv1, 0)

    loads[2].wait()
    loads[5].wait()

    def lay(i, carry):
        rows = wraw[pl.ds(pl.multiple_of(i * 512, 512), 512), :]
        spread = jnp.dot(rows, ewb[...], preferred_element_type=F32)
        wtmp[0] = spread[:, :128]
        wtmp[1] = spread[:, 128:]
        for o in range(16):
            for q in range(2):
                wgt[i, o, q] = (
                    wtmp[0, pl.ds(o * 32 + 2 * q, ML, stride=4), :]
                    + wtmp[1, pl.ds(o * 32 + 2 * q + 1, ML, stride=4), :]
                )
        return carry

    lax.fori_loop(0, 16, lay, 0)
    loads[3].wait()
    loads[4].wait()

    finish(send1, recv1, 0, NS)
    spectra = jnp.dot(wxb[...], recv1[...].reshape(512, 256), preferred_element_type=F32)
    n0, n1 = spectra[:, :128], spectra[:, 128:]
    send2[:, :, :128] = (
        jnp.concatenate([n0[:, :64], n1[:, :64]], 1).astype(BF).reshape(NC, 16, 128)
    )
    send2[:, :, 128:] = (
        jnp.concatenate([n0[:, 64:], n1[:, 64:]], 1).astype(BF).reshape(NC, 16, 128)
    )
    chan_exchange(send2, recv2, 1)
    finish(send2, recv2, 1, NC)

    ins = recv2[...].astype(F32)
    for half in range(NC):
        outs = []
        for o in (2 * half, 2 * half + 1):
            re = jnp.zeros((ML, 128), F32)
            im = jnp.zeros((ML, 128), F32)
            for i in range(16):
                part = ins[i // 2, :, (i % 2) * 128 : (i % 2 + 1) * 128]
                s_re, s_im = part[:ML], part[ML:]
                w_re, w_im = wgt[i, o, 0], wgt[i, o, 1]
                re = re + (s_re * w_re - s_im * w_im)
                im = im + (s_re * w_im + s_im * w_re)
            outs.append(jnp.concatenate([re, im], 0))
        first, second = outs
        send3[half, :, :128] = jnp.concatenate([first[:, :64], second[:, :64]], 1).astype(BF)
        send3[half, :, 128:] = jnp.concatenate([first[:, 64:], second[:, 64:]], 1).astype(BF)
    chan_exchange(send3, recv3, 2)
    finish(send3, recv3, 2, NC)

    back = jnp.dot(ixb[...], recv3[...].reshape(128, 256), preferred_element_type=F32)
    send4[...] = back.astype(BF).reshape(NS, 16, 256)
    slab_exchange(send4, recv4, 3)
    finish(send4, recv4, 3, NS)
    out[...] = recv4[...]
    finish_send(send1, 0, NS)
    finish_send(send2, 1, NC)
    finish_send(send3, 2, NC)
    finish_send(send4, 3, NS)


def inverse_kernel(shift, back, iy, iz, out, wide):
    x = pl.program_id(0)

    @pl.when(x == 0)
    def _():
        full = back[...].reshape(512, 256)
        wide[0] = full[:, :128].astype(F32)
        wide[1] = full[:, 128:].astype(F32)

    rows = [
        wide[h, pl.ds(2 * x + p, NS, stride=16), :].astype(BF) for h in range(2) for p in range(2)
    ]
    cols = jnp.concatenate(rows, 0)
    u = jnp.dot(iy[...], cols, preferred_element_type=F32).astype(BF)
    lhs = jnp.concatenate([u[:NG], u[NG:]], 1)
    for b in range(2):
        for o in range(2):
            v = jnp.dot(lhs, iz[2 * b + o], preferred_element_type=F32) + shift[o]
            out[b, o, 0] = (0.5 * v * (1.0 + lax.erf(v * np.float32(np.sqrt(0.5))))).astype(BF)


def on_device(state_field, spectral_weights, channel_shift):
    wz, wy, wx, ix, iy, iz, ew = make_tables()
    w2d = spectral_weights.transpose(0, 1, 2, 4, 5, 3).reshape(16 * 16 * ML * 4, KM)
    anywhere = pl.BlockSpec(memory_space=pl.ANY)
    vmem = pl.BlockSpec(memory_space=pltpu.VMEM)
    slots, few = (NS, 16, 256), (NC, 16, 256)
    back = pl.pallas_call(
        forward_kernel,
        out_shape=jax.ShapeDtypeStruct(slots, BF),
        in_specs=[anywhere] * 7,
        out_specs=vmem,
        scratch_shapes=[
            pltpu.VMEM((XL, 2, 2, NG, NG), BF),
            pltpu.VMEM(w2d.shape, BF),
            pltpu.VMEM(wz.shape, BF),
            pltpu.VMEM(wy.shape, BF),
            pltpu.VMEM(wx.shape, BF),
            pltpu.VMEM(ix.shape, BF),
            pltpu.VMEM(ew.shape, BF),
            pltpu.VMEM((2, 512, 128), F32),
            pltpu.VMEM((2, 512, 128), F32),
            pltpu.VMEM((16, 16, 2, ML, 128), F32),
            pltpu.VMEM(slots, BF),
            pltpu.VMEM(slots, BF),
            pltpu.VMEM(few, BF),
            pltpu.VMEM(few, BF),
            pltpu.VMEM(few, BF),
            pltpu.VMEM(few, BF),
            pltpu.VMEM(slots, BF),
            pltpu.VMEM(slots, BF),
            pltpu.SemaphoreType.DMA((XL,)),
            pltpu.SemaphoreType.DMA((6,)),
            pltpu.SemaphoreType.DMA((4,)),
            pltpu.SemaphoreType.DMA((4,)),
        ],
        compiler_params=pltpu.CompilerParams(
            collective_id=0, has_side_effects=True, vmem_limit_bytes=40 * 2**20
        ),
    )(state_field, w2d, wz, wy, wx, ix, ew)
    whole = pl.BlockSpec(memory_space=pltpu.VMEM)
    return pl.pallas_call(
        inverse_kernel,
        out_shape=jax.ShapeDtypeStruct((2, 2, XL, NG, NG), BF),
        grid=(XL,),
        in_specs=[pl.BlockSpec(memory_space=pltpu.SMEM), whole, whole, whole],
        out_specs=pl.BlockSpec((2, 2, 1, NG, NG), lambda x: (0, 0, x, 0, 0)),
        scratch_shapes=[pltpu.VMEM((2, 512, 128), F32)],
        compiler_params=pltpu.CompilerParams(vmem_limit_bytes=40 * 2**20),
    )(channel_shift.astype(F32), back, iy, iz)


def solution(mesh):
    return jax.shard_map(
        on_device,
        mesh=mesh,
        in_specs=(
            P(None, "chan", "slab", None, None),
            P(None, None, "chan", None, None, "slab"),
            P("chan"),
        ),
        out_specs=P(None, "chan", "slab", None, None),
        check_vma=False,
    )
```

```python
import jax
import jax.numpy as jnp
import ml_dtypes
import numpy as np
from jax import lax
from jax.experimental import pallas as pl
from jax.experimental.pallas import tpu as pltpu
from jax.sharding import PartitionSpec as P

NG = 256
KM = 32
NS = 32
NC = 8
XL = NG // NS
ML = 2 * KM // NC
F32 = jnp.float32
BF = jnp.bfloat16
MESH = pl.DeviceIdType.MESH
STEPS = sorted(
    ((dy, dz) for dy in range(-1, 3) for dz in range(-3, 5) if (dy, dz) != (0, 0)),
    key=lambda t: (-abs(t[0]), -abs(t[1]), t[1], t[0]),
)


def make_tables():
    j = np.arange(NG)
    f2 = np.arange(2 * KM)
    f2 = np.where(f2 < KM, f2, f2 + NG - 2 * KM)
    unit = np.float32(2.0 * np.pi / NG)
    tz = ((np.arange(KM)[:, None] * j[None, :]) % NG).astype(np.float32) * unit
    t2 = ((f2[:, None] * j[None, :]) % NG).astype(np.float32) * unit
    cz, sz = np.cos(tz), np.sin(tz)
    c2, s2 = np.cos(t2), np.sin(t2)
    fwd, inv = 1.0 / 16.0, 1.0 / 8.0

    wz = np.zeros((2, 2, NG, 2, 2, 2, KM), np.float32)
    for b in range(2):
        for c in range(2):
            wz[b, c, :, 0, c, b, :] = cz.T * fwd
            wz[b, c, :, 1, c, b, :] = -sz.T * fwd
    wz = wz.reshape(4 * NG, 256)
    order = np.concatenate([np.arange(0, 2 * KM, 2), np.arange(1, 2 * KM, 2)])
    wy = np.concatenate([c2[order], s2[order]], 0) * fwd
    c8, s8 = c2.reshape(NC, ML, NG), s2.reshape(NC, ML, NG)
    wx = np.zeros((NC, 2, ML, NG, 2), np.float32)
    wx[:, 0, :, :, 0], wx[:, 0, :, :, 1] = c8, s8
    wx[:, 1, :, :, 0], wx[:, 1, :, :, 1] = -s8, c8
    wx = wx.reshape(2 * 2 * KM, 2 * NG) * fwd
    ix = np.zeros((NG, 2, NC, 2, ML), np.float32)
    ct, st = c8.transpose(2, 0, 1), s8.transpose(2, 0, 1)
    ix[:, 0, :, 0], ix[:, 0, :, 1] = ct, -st
    ix[:, 1, :, 0], ix[:, 1, :, 1] = st, ct
    ix = ix.reshape(2 * NG, 2 * 2 * KM) * inv
    iy = np.zeros((2, NG, 2, 2, KM), np.float32)
    for h in range(2):
        ch, sh = c2[h::2].T, s2[h::2].T
        iy[0, :, h, 0], iy[0, :, h, 1] = ch, -sh
        iy[1, :, h, 0], iy[1, :, h, 1] = sh, ch
    iy = iy.reshape(2 * NG, 4 * KM) * inv
    wk = np.where(np.arange(KM) == 0, 1.0, 2.0)[:, None]
    iz = np.zeros((2, 2, 2, 2, 2, KM, NG), np.float32)
    for b in range(2):
        for o in range(2):
            iz[b, o, 0, o, b] = wk * cz * inv
            iz[b, o, 1, o, b] = -wk * sz * inv
    iz = iz.reshape(4, 256, NG)
    ew = np.zeros((KM, 2, 2, 2, KM), np.float32)
    for h in range(2):
        for b in range(2):
            ew[:, h, h, b, :] = np.eye(KM)
    ew = ew.reshape(KM, 256)
    return tuple(np.asarray(t).astype(ml_dtypes.bfloat16) for t in (wz, wy, wx, ix, iy, iz, ew))


def forward_kernel(
    state, w2d, wz, wy, wx, ix, ew, out,
    xbuf, wraw, wzb, wyb, wxb, ixb, ewb, tmp, wtmp, wgt,
    send1, recv1, send2, recv2, send3, recv3, send4, recv4,
    in_sem, tab_sem, ssem, rsem,
):
    slab = lax.axis_index("slab")
    chan = lax.axis_index("chan")

    loads = []
    for at, (src, dst) in enumerate(
        ((wz, wzb), (wy, wyb), (w2d, wraw), (wx, wxb), (ix, ixb), (ew, ewb))
    ):
        loads.append(pltpu.make_async_copy(src, dst, tab_sem.at[at]))
    planes = [
        pltpu.make_async_copy(state.at[:, :, x], xbuf.at[x], in_sem.at[x]) for x in range(XL)
    ]
    loads[0].start()
    planes[0].start()
    loads[1].start()
    for x in range(1, XL):
        planes[x].start()
    for at in range(2, 6):
        loads[at].start()

    barrier = pltpu.get_barrier_semaphore()

    def greet_slab(j, carry):
        pl.semaphore_signal(
            barrier, inc=1, device_id=(lax.rem(slab + j, NS), chan), device_id_type=MESH
        )
        return carry

    def greet_chan(j, carry):
        pl.semaphore_signal(
            barrier, inc=1, device_id=(slab, lax.rem(chan + j, NC)), device_id_type=MESH
        )
        return carry

    lax.fori_loop(1, NS, greet_slab, 0)
    lax.fori_loop(1, NC, greet_chan, 0)

    loads[0].wait()
    loads[1].wait()
    for x in range(XL):
        planes[x].wait()
        four = jnp.concatenate([xbuf[x, b, c] for b in range(2) for c in range(2)], axis=1)
        coef_z = jnp.dot(four, wzb[...], preferred_element_type=F32).astype(BF)
        u = jnp.dot(wyb[...], coef_z, preferred_element_type=F32)
        re = u[:64, :128] + u[64:, 128:]
        im = u[:64, 128:] - u[64:, :128]
        for h in range(2):
            tmp[h, pl.ds(2 * x, NS, stride=16), :] = re[h * NS : (h + 1) * NS]
            tmp[h, pl.ds(2 * x + 1, NS, stride=16), :] = im[h * NS : (h + 1) * NS]
    for h in range(2):
        send1[:, :, h * 128 : (h + 1) * 128] = tmp[h].astype(BF).reshape(NS, 16, 128)

    pl.semaphore_wait(barrier, NS - 1 + NC - 1)

    def slab_exchange(send, recv, at):
        for dy, dz in STEPS:
            peer = lax.rem(slab // 8 + dy + 4, 4) * 8 + lax.rem(lax.rem(slab, 8) + dz + 8, 8)
            pltpu.make_async_remote_copy(
                src_ref=send.at[peer],
                dst_ref=recv.at[slab],
                send_sem=ssem.at[at],
                recv_sem=rsem.at[at],
                device_id=(peer, chan),
                device_id_type=MESH,
            ).start()
        recv[slab] = send[slab]

    def chan_exchange(send, recv, at):
        def post(j, carry):
            peer = lax.rem(chan + j, NC)
            pltpu.make_async_remote_copy(
                src_ref=send.at[peer],
                dst_ref=recv.at[chan],
                send_sem=ssem.at[at],
                recv_sem=rsem.at[at],
                device_id=(slab, peer),
                device_id_type=MESH,
            ).start()
            return carry

        lax.fori_loop(1, NC, post, 0)
        recv[chan] = send[chan]

    def finish(send, recv, at, n):
        some = pl.ds(0, n - 1)
        pltpu.make_async_copy(recv.at[some], recv.at[some], rsem.at[at]).wait()

    def finish_send(send, at, n):
        some = pl.ds(0, n - 1)
        pltpu.make_async_copy(send.at[some], send.at[some], ssem.at[at]).wait()

    slab_exchange(send1, recv1, 0)

    loads[2].wait()
    loads[5].wait()

    def lay(i, carry):
        rows = wraw[pl.ds(pl.multiple_of(i * 512, 512), 512), :]
        spread = jnp.dot(rows, ewb[...], preferred_element_type=F32)
        wtmp[0] = spread[:, :128]
        wtmp[1] = spread[:, 128:]
        for o in range(16):
            for q in range(2):
                wgt[i, o, q] = (
                    wtmp[0, pl.ds(o * 32 + 2 * q, ML, stride=4), :]
                    + wtmp[1, pl.ds(o * 32 + 2 * q + 1, ML, stride=4), :]
                )
        return carry

    lax.fori_loop(0, 16, lay, 0)
    loads[3].wait()
    loads[4].wait()

    finish(send1, recv1, 0, NS)
    spectra = jnp.dot(wxb[...], recv1[...].reshape(512, 256), preferred_element_type=F32)
    n0, n1 = spectra[:, :128], spectra[:, 128:]
    send2[:, :, :128] = (
        jnp.concatenate([n0[:, :64], n1[:, :64]], 1).astype(BF).reshape(NC, 16, 128)
    )
    send2[:, :, 128:] = (
        jnp.concatenate([n0[:, 64:], n1[:, 64:]], 1).astype(BF).reshape(NC, 16, 128)
    )
    chan_exchange(send2, recv2, 1)
    finish(send2, recv2, 1, NC)

    ins = recv2[...].astype(F32)
    for half in range(NC):
        outs = []
        for o in (2 * half, 2 * half + 1):
            re = jnp.zeros((ML, 128), F32)
            im = jnp.zeros((ML, 128), F32)
            for i in range(16):
                part = ins[i // 2, :, (i % 2) * 128 : (i % 2 + 1) * 128]
                s_re, s_im = part[:ML], part[ML:]
                w_re, w_im = wgt[i, o, 0], wgt[i, o, 1]
                re = re + (s_re * w_re - s_im * w_im)
                im = im + (s_re * w_im + s_im * w_re)
            outs.append(jnp.concatenate([re, im], 0))
        first, second = outs
        send3[half, :, :128] = jnp.concatenate([first[:, :64], second[:, :64]], 1).astype(BF)
        send3[half, :, 128:] = jnp.concatenate([first[:, 64:], second[:, 64:]], 1).astype(BF)
    chan_exchange(send3, recv3, 2)
    finish(send3, recv3, 2, NC)

    back = jnp.dot(ixb[...], recv3[...].reshape(128, 256), preferred_element_type=F32)
    send4[...] = back.astype(BF).reshape(NS, 16, 256)
    slab_exchange(send4, recv4, 3)
    finish(send4, recv4, 3, NS)
    out[...] = recv4[...]
    finish_send(send1, 0, NS)
    finish_send(send2, 1, NC)
    finish_send(send3, 2, NC)
    finish_send(send4, 3, NS)


def inverse_kernel(shift, back, iy, iz, out, wide):
    x = pl.program_id(0)

    @pl.when(x == 0)
    def _():
        full = back[...].reshape(512, 256)
        wide[0] = full[:, :128].astype(F32)
        wide[1] = full[:, 128:].astype(F32)

    rows = [
        wide[h, pl.ds(2 * x + p, NS, stride=16), :].astype(BF) for h in range(2) for p in range(2)
    ]
    cols = jnp.concatenate(rows, 0)
    u = jnp.dot(iy[...], cols, preferred_element_type=F32).astype(BF)
    lhs = jnp.concatenate([u[:NG], u[NG:]], 1)
    for b in range(2):
        for o in range(2):
            v = jnp.dot(lhs, iz[2 * b + o], preferred_element_type=F32) + shift[o]
            out[b, o, 0] = (0.5 * v * (1.0 + lax.erf(v * np.float32(np.sqrt(0.5))))).astype(BF)


def on_device(state_field, spectral_weights, channel_shift):
    wz, wy, wx, ix, iy, iz, ew = make_tables()
    w2d = spectral_weights.transpose(0, 1, 2, 4, 5, 3).reshape(16 * 16 * ML * 4, KM)
    anywhere = pl.BlockSpec(memory_space=pltpu.HBM)
    vmem = pl.BlockSpec(memory_space=pltpu.VMEM)
    slots, few = (NS, 16, 256), (NC, 16, 256)
    operands = (state_field, w2d, wz, wy, wx, ix, ew)
    back = pl.pallas_call(
        forward_kernel,
        out_shape=jax.ShapeDtypeStruct(slots, BF),
        in_specs=[anywhere] * 7,
        out_specs=vmem,
        scratch_shapes=[
            pltpu.VMEM((XL, 2, 2, NG, NG), BF),
            pltpu.VMEM(w2d.shape, BF),
            pltpu.VMEM(wz.shape, BF),
            pltpu.VMEM(wy.shape, BF),
            pltpu.VMEM(wx.shape, BF),
            pltpu.VMEM(ix.shape, BF),
            pltpu.VMEM(ew.shape, BF),
            pltpu.VMEM((2, 512, 128), F32),
            pltpu.VMEM((2, 512, 128), F32),
            pltpu.VMEM((16, 16, 2, ML, 128), F32),
            pltpu.VMEM(slots, BF),
            pltpu.VMEM(slots, BF),
            pltpu.VMEM(few, BF),
            pltpu.VMEM(few, BF),
            pltpu.VMEM(few, BF),
            pltpu.VMEM(few, BF),
            pltpu.VMEM(slots, BF),
            pltpu.VMEM(slots, BF),
            pltpu.SemaphoreType.DMA((XL,)),
            pltpu.SemaphoreType.DMA((6,)),
            pltpu.SemaphoreType.DMA((4,)),
            pltpu.SemaphoreType.DMA((4,)),
        ],
        compiler_params=pltpu.CompilerParams(
            collective_id=0, has_side_effects=True, vmem_limit_bytes=40 * 2**20
        ),
    )(*[pltpu.with_memory_space_constraint(v, pltpu.HBM) for v in operands])
    whole = pl.BlockSpec(memory_space=pltpu.VMEM)
    return pl.pallas_call(
        inverse_kernel,
        out_shape=jax.ShapeDtypeStruct((2, 2, XL, NG, NG), BF),
        grid=(XL,),
        in_specs=[pl.BlockSpec(memory_space=pltpu.SMEM), whole, whole, whole],
        out_specs=pl.BlockSpec((2, 2, 1, NG, NG), lambda x: (0, 0, x, 0, 0)),
        scratch_shapes=[pltpu.VMEM((2, 512, 128), F32)],
        compiler_params=pltpu.CompilerParams(vmem_limit_bytes=40 * 2**20),
    )(channel_shift.astype(F32), back, iy, iz)


def solution(mesh):
    return jax.shard_map(
        on_device,
        mesh=mesh,
        in_specs=(
            P(None, "chan", "slab", None, None),
            P(None, None, "chan", None, None, "slab"),
            P("chan"),
        ),
        out_specs=P(None, "chan", "slab", None, None),
        check_vma=False,
    )
```

```python
import jax
import jax.numpy as jnp
import ml_dtypes
import numpy as np
from jax import lax
from jax.experimental import pallas as pl
from jax.experimental.pallas import tpu as pltpu
from jax.sharding import PartitionSpec as P

NG = 256
KM = 32
NS = 32
NC = 8
XL = NG // NS
ML = 2 * KM // NC
F32 = jnp.float32
BF = jnp.bfloat16
MESH = pl.DeviceIdType.MESH
STEPS = sorted(
    ((dy, dz) for dy in range(-1, 3) for dz in range(-3, 5) if (dy, dz) != (0, 0)),
    key=lambda t: (-abs(t[0]), -abs(t[1]), t[1], t[0]),
)


def make_tables():
    j = np.arange(NG)
    f2 = np.arange(2 * KM)
    f2 = np.where(f2 < KM, f2, f2 + NG - 2 * KM)
    unit = np.float32(2.0 * np.pi / NG)
    tz = ((np.arange(KM)[:, None] * j[None, :]) % NG).astype(np.float32) * unit
    t2 = ((f2[:, None] * j[None, :]) % NG).astype(np.float32) * unit
    cz, sz = np.cos(tz), np.sin(tz)
    c2, s2 = np.cos(t2), np.sin(t2)
    fwd, inv = 1.0 / 16.0, 1.0 / 8.0

    wz = np.zeros((2, 2, NG, 2, 2, 2, KM), np.float32)
    for x in range(2):
        for c in range(2):
            wz[x, c, :, 0, x, c, :] = cz.T * fwd
            wz[x, c, :, 1, x, c, :] = -sz.T * fwd
    wz = wz.reshape(4 * NG, 256)
    order = np.concatenate([np.arange(0, 2 * KM, 2), np.arange(1, 2 * KM, 2)])
    wy = np.concatenate([c2[order], s2[order]], 0) * fwd
    c8, s8 = c2.reshape(NC, ML, NG), s2.reshape(NC, ML, NG)
    wx = np.zeros((NC, 2, ML, NG, 2), np.float32)
    wx[:, 0, :, :, 0], wx[:, 0, :, :, 1] = c8, s8
    wx[:, 1, :, :, 0], wx[:, 1, :, :, 1] = -s8, c8
    wx = wx.reshape(2 * 2 * KM, 2 * NG) * fwd
    ix = np.zeros((NG, 2, NC, 2, ML), np.float32)
    ct, st = c8.transpose(2, 0, 1), s8.transpose(2, 0, 1)
    ix[:, 0, :, 0], ix[:, 0, :, 1] = ct, -st
    ix[:, 1, :, 0], ix[:, 1, :, 1] = st, ct
    ix = ix.reshape(2 * NG, 2 * 2 * KM) * inv
    iy = np.zeros((2, NG, 2, 2, KM), np.float32)
    for h in range(2):
        ch, sh = c2[h::2].T, s2[h::2].T
        iy[0, :, h, 0], iy[0, :, h, 1] = ch, -sh
        iy[1, :, h, 0], iy[1, :, h, 1] = sh, ch
    iy = iy.reshape(2 * NG, 4 * KM) * inv
    wk = np.where(np.arange(KM) == 0, 1.0, 2.0)[:, None]
    iz = np.zeros((2, 2, 2, 2, 2, KM, NG), np.float32)
    for x in range(2):
        for o in range(2):
            iz[x, o, 0, x, o] = wk * cz * inv
            iz[x, o, 1, x, o] = -wk * sz * inv
    iz = iz.reshape(4, 256, NG)
    ew = np.zeros((2, KM, 2, 2, 2, KM), np.float32)
    for c in range(2):
        for h in range(2):
            ew[c, :, h, h, c, :] = np.eye(KM)
    ew = ew.reshape(2, KM, 256)
    return tuple(np.asarray(t).astype(ml_dtypes.bfloat16) for t in (wz, wy, wx, ix, iy, iz, ew))


def split_halves(first, second):
    return (
        jnp.concatenate([first[:, :64], second[:, :64]], 1),
        jnp.concatenate([first[:, 64:], second[:, 64:]], 1),
    )


def inverse_pair(pair, wide, iy, iz, shift, put):
    parts = []
    for p in range(2):
        a = wide[pl.ds(4 * pair + p, NS, stride=16), :]
        b = wide[pl.ds(4 * pair + 2 + p, NS, stride=16), :]
        parts.append(split_halves(a, b))
    cols = jnp.concatenate([parts[p][h] for h in range(2) for p in range(2)], 0).astype(BF)
    u = jnp.dot(iy[...], cols, preferred_element_type=F32).astype(BF)
    lhs = jnp.concatenate([u[:NG], u[NG:]], 1)
    for x in range(2):
        for o in range(2):
            v = jnp.dot(lhs, iz[2 * x + o], preferred_element_type=F32) + shift[:, o : o + 1]
            put(o, 2 * pair + x, (0.5 * v * (1.0 + lax.erf(v * np.float32(np.sqrt(0.5))))).astype(BF))


def forward_kernel(
    state, w2d, wz, wy, wx, ix, ew, iy, iz, shift, done0, back1, bias,
    sbuf, xbuf, wraw, wzb, wyb, wxb, ixb, ewb, iyb, izb, tmp, wtmp, wgt,
    send1, recv1, send2, recv2, send3, recv3, send4, recv4, obuf,
    in_sem, tab_sem, out_sem, ssem, rsem,
):
    slab = lax.axis_index("slab")
    chan = lax.axis_index("chan")

    tables = ((wz, wzb), (wy, wyb), (w2d, wraw), (wx, wxb), (ix, ixb), (ew, ewb), (iy, iyb), (iz, izb), (shift, sbuf))
    loads = [pltpu.make_async_copy(src, dst, tab_sem.at[at]) for at, (src, dst) in enumerate(tables)]
    planes = [
        [
            pltpu.make_async_copy(
                state.at[b, c, pl.ds(4 * h, 4)], xbuf.at[b, c, pl.ds(4 * h, 4)], in_sem.at[b, h, c]
            )
            for h in range(2)
            for c in range(2)
        ]
        for b in range(2)
    ]
    loads[0].start()
    for copy in planes[0]:
        copy.start()
    loads[1].start()
    for copy in planes[1]:
        copy.start()
    for at in (2, 5, 3, 4, 6, 7, 8):
        loads[at].start()

    barrier = pltpu.get_barrier_semaphore()

    def greet_slab(j, carry):
        pl.semaphore_signal(
            barrier, inc=1, device_id=(lax.rem(slab + j, NS), chan), device_id_type=MESH
        )
        return carry

    def greet_chan(j, carry):
        pl.semaphore_signal(
            barrier, inc=1, device_id=(slab, lax.rem(chan + j, NC)), device_id_type=MESH
        )
        return carry

    lax.fori_loop(1, NS, greet_slab, 0)
    lax.fori_loop(1, NC, greet_chan, 0)

    def slab_exchange(send, recv, at, b):
        for dy, dz in STEPS:
            peer = lax.rem(slab // 8 + dy + 4, 4) * 8 + lax.rem(lax.rem(slab, 8) + dz + 8, 8)
            pltpu.make_async_remote_copy(
                src_ref=send.at[b, peer],
                dst_ref=recv.at[b, slab],
                send_sem=ssem.at[at, b],
                recv_sem=rsem.at[at, b],
                device_id=(peer, chan),
                device_id_type=MESH,
            ).start()
        recv[b, slab] = send[b, slab]

    def chan_exchange(send, recv, at, b):
        for j in (4, 5, 3, 2, 6, 7, 1):
            peer = lax.rem(chan + j, NC)
            pltpu.make_async_remote_copy(
                src_ref=send.at[b, peer],
                dst_ref=recv.at[b, chan],
                send_sem=ssem.at[at, b],
                recv_sem=rsem.at[at, b],
                device_id=(slab, peer),
                device_id_type=MESH,
            ).start()
        recv[b, chan] = send[b, chan]

    def finish(recv, at, b, n):
        some = recv.at[b, pl.ds(0, n - 1)]
        pltpu.make_async_copy(some, some, rsem.at[at, b]).wait()

    def finish_send(send, at, b, n):
        some = send.at[b, pl.ds(0, n - 1)]
        pltpu.make_async_copy(some, some, ssem.at[at, b]).wait()

    loads[0].wait()
    for b in range(2):
        for h in range(2):
            for copy in planes[b][2 * h : 2 * h + 2]:
                copy.wait()
            if b == 0 and h == 0:
                loads[1].wait()
            for pair in (2 * h, 2 * h + 1):
                four = jnp.concatenate(
                    [xbuf[b, c, 2 * pair + x] for x in range(2) for c in range(2)], axis=1
                )
                coef_z = jnp.dot(four, wzb[...], preferred_element_type=F32).astype(BF)
                u = jnp.dot(wyb[...], coef_z, preferred_element_type=F32)
                re = u[:64, :128] + u[64:, 128:]
                im = u[:64, 128:] - u[64:, :128]
                for q, val in enumerate((re, im)):
                    for x, rows in enumerate(split_halves(val[:NS], val[NS:])):
                        tmp[pl.ds(2 * (2 * pair + x) + q, NS, stride=16), :] = rows
        send1[b] = tmp[...].astype(BF).reshape(NS, 16, 128)
        if b == 0:
            pl.semaphore_wait(barrier, NS - 1 + NC - 1)
        slab_exchange(send1, recv1, 0, b)

    loads[2].wait()
    loads[5].wait()

    def lay(i, carry):
        even = wraw[pl.ds(pl.multiple_of(i * 1024, 512), 512), :]
        odd = wraw[pl.ds(pl.multiple_of(i * 1024 + 512, 512), 512), :]
        spread = jnp.dot(even, ewb[0], preferred_element_type=F32) + jnp.dot(
            odd, ewb[1], preferred_element_type=F32
        )
        wtmp[0] = spread[:, :128]
        wtmp[1] = spread[:, 128:]
        for o in range(16):
            for q in range(2):
                wgt[i, o, q] = (
                    wtmp[0, pl.ds(o * 32 + 2 * q, ML, stride=4), :]
                    + wtmp[1, pl.ds(o * 32 + 2 * q + 1, ML, stride=4), :]
                )
        return carry

    lax.fori_loop(0, NC, lay, 0)
    for at in (3, 4, 6, 7, 8):
        loads[at].wait()

    for b in range(2):
        finish(recv1, 0, b, NS)
        spectra = jnp.dot(wxb[...], recv1[b].reshape(512, 128), preferred_element_type=F32)
        send2[b] = spectra.astype(BF).reshape(NC, 16, 128)
        chan_exchange(send2, recv2, 1, b)

    low = lax.rem(lax.broadcasted_iota(jnp.int32, (2 * ML, 128), 1), 64) < KM
    for b in range(2):
        finish(recv2, 1, b, NC)
        ins = recv2[b].astype(F32)
        for half in range(NC):
            outs = []
            for o in (2 * half, 2 * half + 1):
                re = jnp.zeros((ML, 128), F32)
                im = jnp.zeros((ML, 128), F32)
                for i in range(NC):
                    s_re, s_im = ins[i, :ML], ins[i, ML:]
                    w_re, w_im = wgt[i, o, 0], wgt[i, o, 1]
                    re = re + (s_re * w_re - s_im * w_im)
                    im = im + (s_re * w_im + s_im * w_re)
                both = jnp.concatenate([re, im], 0)
                outs.append(both + pltpu.roll(both, 128 - KM if o % 2 == 0 else KM, 1))
            send3[b, half] = jnp.where(low, outs[0], outs[1]).astype(BF)
        chan_exchange(send3, recv3, 2, b)

    for b in range(2):
        finish(recv3, 2, b, NC)
        back = jnp.dot(ixb[...], recv3[b].reshape(128, 128), preferred_element_type=F32)
        send4[b] = back.astype(BF).reshape(NS, 16, 128)
        slab_exchange(send4, recv4, 3, b)

    bias[...] = sbuf[...].astype(F32)
    finish(recv4, 3, 0, NS)
    tmp[...] = recv4[0].reshape(512, 128).astype(F32)

    def put(o, x, v):
        obuf[o, x] = v

    def result(pair):
        two = pl.ds(2 * pair, 2)
        return pltpu.make_async_copy(obuf.at[:, two], done0.at[:, two], out_sem.at[pair])

    def inverse(pair, carry):
        inverse_pair(pair, tmp, iyb, izb, bias[...], put)
        result(pair).start()
        return carry

    lax.fori_loop(0, XL // 2, inverse, 0)
    finish(recv4, 3, 1, NS)
    back1[...] = recv4[1]
    for b in range(2):
        finish_send(send1, 0, b, NS)
        finish_send(send2, 1, b, NC)
        finish_send(send3, 2, b, NC)
        finish_send(send4, 3, b, NS)
    for pair in range(XL // 2):
        result(pair).wait()


def inverse_kernel(bias, done0, back1, iy, iz, out, tmp, obuf, sem, out_sem):
    half = pltpu.make_async_copy(done0, out.at[0], sem)
    half.start()
    tmp[...] = back1[...].reshape(512, 128).astype(F32)

    def put(o, x, v):
        obuf[o, x] = v

    def result(pair):
        two = pl.ds(2 * pair, 2)
        return pltpu.make_async_copy(obuf.at[:, two], out.at[1, :, two], out_sem.at[pair])

    def inverse(pair, carry):
        inverse_pair(pair, tmp, iy, iz, bias[...], put)
        result(pair).start()
        return carry

    lax.fori_loop(0, XL // 2, inverse, 0)
    for pair in range(XL // 2):
        result(pair).wait()
    half.wait()


def on_device(state_field, spectral_weights, channel_shift):
    wz, wy, wx, ix, iy, iz, ew = make_tables()
    w2d = spectral_weights.transpose(0, 1, 2, 4, 5, 3).reshape(16 * 16 * ML * 4, KM)
    shift = channel_shift.reshape(1, 2)
    anywhere = pl.BlockSpec(memory_space=pltpu.HBM)
    vmem = pl.BlockSpec(memory_space=pltpu.VMEM)
    slots, few = (2, NS, 16, 128), (2, NC, 16, 128)
    planes = (2, XL, NG, NG)
    operands = (state_field, w2d, wz, wy, wx, ix, ew, iy, iz, shift)
    done0, back1, bias = pl.pallas_call(
        forward_kernel,
        out_shape=(
            jax.ShapeDtypeStruct(planes, BF),
            jax.ShapeDtypeStruct(slots[1:], BF),
            jax.ShapeDtypeStruct((1, 2), F32),
        ),
        in_specs=[anywhere] * len(operands),
        out_specs=(anywhere, vmem, vmem),
        scratch_shapes=[
            pltpu.VMEM((1, 2), BF),
            pltpu.VMEM((2, *planes), BF),
            *[pltpu.VMEM(t.shape, BF) for t in (w2d, wz, wy, wx, ix, ew, iy, iz)],
            pltpu.VMEM((512, 128), F32),
            pltpu.VMEM((2, 512, 128), F32),
            pltpu.VMEM((NC, 16, 2, ML, 128), F32),
            *[pltpu.VMEM(s, BF) for s in (slots, slots, few, few, few, few, slots, slots)],
            pltpu.VMEM(planes, BF),
            pltpu.SemaphoreType.DMA((2, 2, 2)),
            pltpu.SemaphoreType.DMA((9,)),
            pltpu.SemaphoreType.DMA((XL // 2,)),
            pltpu.SemaphoreType.DMA((4, 2)),
            pltpu.SemaphoreType.DMA((4, 2)),
        ],
        compiler_params=pltpu.CompilerParams(
            collective_id=0, has_side_effects=True, vmem_limit_bytes=40 * 2**20
        ),
    )(*[pltpu.with_memory_space_constraint(v, pltpu.HBM) for v in operands])
    return pl.pallas_call(
        inverse_kernel,
        out_shape=jax.ShapeDtypeStruct((2, *planes), BF),
        in_specs=[vmem, anywhere, vmem, vmem, vmem],
        out_specs=anywhere,
        scratch_shapes=[
            pltpu.VMEM((512, 128), F32),
            pltpu.VMEM(planes, BF),
            pltpu.SemaphoreType.DMA,
            pltpu.SemaphoreType.DMA((XL // 2,)),
        ],
        compiler_params=pltpu.CompilerParams(vmem_limit_bytes=40 * 2**20),
    )(bias, done0, back1, iy, iz)


def solution(mesh):
    return jax.shard_map(
        on_device,
        mesh=mesh,
        in_specs=(
            P(None, "chan", "slab", None, None),
            P(None, None, "chan", None, None, "slab"),
            P("chan"),
        ),
        out_specs=P(None, "chan", "slab", None, None),
        check_vma=False,
    )
```

```python
import jax
import jax.numpy as jnp
import ml_dtypes
import numpy as np
from jax import lax
from jax.experimental import pallas as pl
from jax.experimental.pallas import tpu as pltpu
from jax.sharding import PartitionSpec as P

NG = 256
KM = 32
NS = 32
NC = 8
XL = NG // NS
ML = 2 * KM // NC
F32 = jnp.float32
BF = jnp.bfloat16
MESH = pl.DeviceIdType.MESH
STEPS = sorted(
    ((dy, dz) for dy in range(-1, 3) for dz in range(-3, 5) if (dy, dz) != (0, 0)),
    key=lambda t: (-abs(t[0]), -abs(t[1]), t[1], t[0]),
)


def make_tables():
    j = np.arange(NG)
    f2 = np.arange(2 * KM)
    f2 = np.where(f2 < KM, f2, f2 + NG - 2 * KM)
    unit = np.float32(2.0 * np.pi / NG)
    tz = ((np.arange(KM)[:, None] * j[None, :]) % NG).astype(np.float32) * unit
    t2 = ((f2[:, None] * j[None, :]) % NG).astype(np.float32) * unit
    cz, sz = np.cos(tz), np.sin(tz)
    c2, s2 = np.cos(t2), np.sin(t2)
    fwd, inv = 1.0 / 16.0, 1.0 / 8.0

    wz = np.zeros((2, 2, NG, 2, 2, 2, KM), np.float32)
    for x in range(2):
        for c in range(2):
            wz[x, c, :, 0, x, c, :] = cz.T * fwd
            wz[x, c, :, 1, x, c, :] = -sz.T * fwd
    wz = wz.reshape(4 * NG, 256)
    order = np.concatenate([np.arange(0, 2 * KM, 2), np.arange(1, 2 * KM, 2)])
    wy = np.concatenate([c2[order], s2[order]], 0) * fwd
    c8, s8 = c2.reshape(NC, ML, NG), s2.reshape(NC, ML, NG)
    wx = np.zeros((NC, 2, ML, NG, 2), np.float32)
    wx[:, 0, :, :, 0], wx[:, 0, :, :, 1] = c8, s8
    wx[:, 1, :, :, 0], wx[:, 1, :, :, 1] = -s8, c8
    wx = wx.reshape(2 * 2 * KM, 2 * NG) * fwd
    ix = np.zeros((NG, 2, NC, 2, ML), np.float32)
    ct, st = c8.transpose(2, 0, 1), s8.transpose(2, 0, 1)
    ix[:, 0, :, 0], ix[:, 0, :, 1] = ct, -st
    ix[:, 1, :, 0], ix[:, 1, :, 1] = st, ct
    ix = ix.reshape(2 * NG, 2 * 2 * KM) * inv
    iy = np.zeros((2, NG, 2, 2, KM), np.float32)
    for h in range(2):
        ch, sh = c2[h::2].T, s2[h::2].T
        iy[0, :, h, 0], iy[0, :, h, 1] = ch, -sh
        iy[1, :, h, 0], iy[1, :, h, 1] = sh, ch
    iy = iy.reshape(2 * NG, 4 * KM) * inv
    wk = np.where(np.arange(KM) == 0, 1.0, 2.0)[:, None]
    iz = np.zeros((2, 2, 2, 2, 2, KM, NG), np.float32)
    for x in range(2):
        for o in range(2):
            iz[x, o, 0, x, o] = wk * cz * inv
            iz[x, o, 1, x, o] = -wk * sz * inv
    iz = iz.reshape(4, 256, NG)
    ew = np.zeros((2, KM, 2, 2, 2, KM), np.float32)
    for c in range(2):
        for h in range(2):
            ew[c, :, h, h, c, :] = np.eye(KM)
    ew = ew.reshape(2, KM, 256)
    return tuple(np.asarray(t).astype(ml_dtypes.bfloat16) for t in (wz, wy, wx, ix, iy, iz, ew))


def split_halves(first, second):
    return (
        jnp.concatenate([first[:, :64], second[:, :64]], 1),
        jnp.concatenate([first[:, 64:], second[:, 64:]], 1),
    )


def inverse(wide, lhs, iy, iz, shift, obuf, sent):
    cols = []
    for pair in range(XL // 2):
        parts = []
        for p in range(2):
            a = wide[pl.ds(4 * pair + p, NS, stride=16), :]
            b = wide[pl.ds(4 * pair + 2 + p, NS, stride=16), :]
            parts.append(split_halves(a, b))
        cols.append(jnp.concatenate([parts[p][h] for h in range(2) for p in range(2)], 0))
    cols = jnp.concatenate(cols, 1).astype(BF)
    u = jnp.dot(iy[...], cols, preferred_element_type=F32).astype(BF)
    for pair in range(XL // 2):
        for q in range(2):
            lhs[pair * NG : (pair + 1) * NG, q * 128 : (q + 1) * 128] = u[
                q * NG : (q + 1) * NG, pair * 128 : (pair + 1) * 128
            ]
    for x in range(2):
        for o in range(2):
            for h in range(2):
                v = jnp.dot(
                    lhs[2 * h * NG : 2 * (h + 1) * NG, :], iz[2 * x + o], preferred_element_type=F32
                )
                v = v + shift[:, o : o + 1]
                v = (0.5 * v * (1.0 + lax.erf(v * np.float32(np.sqrt(0.5))))).astype(BF)
                for at in range(2):
                    obuf[o, 2 * h + at, x] = v[at * NG : (at + 1) * NG]
            sent(o, x).start()


def forward_kernel(
    state, w2d, wz, wy, wx, ix, ew, iy, iz, shift, done0, back1, bias,
    sbuf, xbuf, wraw, wzb, wyb, wxb, ixb, ewb, iyb, izb, tmp, wtmp, wgt,
    send1, recv1, send2, recv2, send3, recv3, send4, recv4, lhs, obuf,
    in_sem, tab_sem, out_sem, ssem, rsem,
):
    slab = lax.axis_index("slab")
    chan = lax.axis_index("chan")

    tables = ((wz, wzb), (wy, wyb), (w2d, wraw), (wx, wxb), (ix, ixb), (ew, ewb), (iy, iyb), (iz, izb), (shift, sbuf))
    loads = [pltpu.make_async_copy(src, dst, tab_sem.at[at]) for at, (src, dst) in enumerate(tables)]
    planes = [
        [
            pltpu.make_async_copy(
                state.at[b, c, pl.ds(4 * h, 4)], xbuf.at[b, c, pl.ds(4 * h, 4)], in_sem.at[b, h, c]
            )
            for h in range(2)
            for c in range(2)
        ]
        for b in range(2)
    ]
    loads[0].start()
    for copy in planes[0]:
        copy.start()
    loads[1].start()
    for copy in planes[1]:
        copy.start()
    for at in (2, 5, 3, 4, 6, 7, 8):
        loads[at].start()

    barrier = pltpu.get_barrier_semaphore()

    def greet_slab(j, carry):
        pl.semaphore_signal(
            barrier, inc=1, device_id=(lax.rem(slab + j, NS), chan), device_id_type=MESH
        )
        return carry

    def greet_chan(j, carry):
        pl.semaphore_signal(
            barrier, inc=1, device_id=(slab, lax.rem(chan + j, NC)), device_id_type=MESH
        )
        return carry

    lax.fori_loop(1, NS, greet_slab, 0)
    lax.fori_loop(1, NC, greet_chan, 0)

    def slab_exchange(send, recv, at, b):
        for dy, dz in STEPS:
            peer = lax.rem(slab // 8 + dy + 4, 4) * 8 + lax.rem(lax.rem(slab, 8) + dz + 8, 8)
            pltpu.make_async_remote_copy(
                src_ref=send.at[b, peer],
                dst_ref=recv.at[b, slab],
                send_sem=ssem.at[at, b],
                recv_sem=rsem.at[at, b],
                device_id=(peer, chan),
                device_id_type=MESH,
            ).start()
        recv[b, slab] = send[b, slab]

    def chan_exchange(send, recv, at, b):
        for j in (4, 5, 3, 2, 6, 7, 1):
            peer = lax.rem(chan + j, NC)
            pltpu.make_async_remote_copy(
                src_ref=send.at[b, peer],
                dst_ref=recv.at[b, chan],
                send_sem=ssem.at[at, b],
                recv_sem=rsem.at[at, b],
                device_id=(slab, peer),
                device_id_type=MESH,
            ).start()
        recv[b, chan] = send[b, chan]

    def finish(recv, at, b, n):
        some = recv.at[b, pl.ds(0, n - 1)]
        pltpu.make_async_copy(some, some, rsem.at[at, b]).wait()

    def finish_send(send, at, b, n):
        some = send.at[b, pl.ds(0, n - 1)]
        pltpu.make_async_copy(some, some, ssem.at[at, b]).wait()

    loads[0].wait()
    for b in range(2):
        for h in range(2):
            for copy in planes[b][2 * h : 2 * h + 2]:
                copy.wait()
            if b == 0 and h == 0:
                loads[1].wait()
            pairs = (2 * h, 2 * h + 1)
            fours = [
                jnp.concatenate([xbuf[b, c, 2 * pair + x] for x in range(2) for c in range(2)], 1)
                for pair in pairs
            ]
            coef_z = jnp.dot(
                jnp.concatenate(fours, 0), wzb[...], preferred_element_type=F32
            ).astype(BF)
            for at, pair in enumerate(pairs):
                u = jnp.dot(
                    wyb[...], coef_z[at * NG : (at + 1) * NG], preferred_element_type=F32
                )
                re = u[:64, :128] + u[64:, 128:]
                im = u[:64, 128:] - u[64:, :128]
                for q, val in enumerate((re, im)):
                    for x, rows in enumerate(split_halves(val[:NS], val[NS:])):
                        tmp[pl.ds(2 * (2 * pair + x) + q, NS, stride=16), :] = rows
        send1[b] = tmp[...].astype(BF).reshape(NS, 16, 128)
        if b == 0:
            pl.semaphore_wait(barrier, NS - 1 + NC - 1)
        slab_exchange(send1, recv1, 0, b)

    loads[2].wait()
    loads[5].wait()

    def lay(i, carry):
        even = wraw[pl.ds(pl.multiple_of(i * 1024, 512), 512), :]
        odd = wraw[pl.ds(pl.multiple_of(i * 1024 + 512, 512), 512), :]
        spread = jnp.dot(even, ewb[0], preferred_element_type=F32) + jnp.dot(
            odd, ewb[1], preferred_element_type=F32
        )
        wtmp[0] = spread[:, :128]
        wtmp[1] = spread[:, 128:]
        for o in range(16):
            for q in range(2):
                wgt[i, o, q] = (
                    wtmp[0, pl.ds(o * 32 + 2 * q, ML, stride=4), :]
                    + wtmp[1, pl.ds(o * 32 + 2 * q + 1, ML, stride=4), :]
                )
        return carry

    lax.fori_loop(0, NC, lay, 0)
    for at in (3, 4, 6, 7, 8):
        loads[at].wait()

    for b in range(2):
        finish(recv1, 0, b, NS)
        spectra = jnp.dot(wxb[...], recv1[b].reshape(512, 128), preferred_element_type=F32)
        send2[b] = spectra.astype(BF).reshape(NC, 16, 128)
        chan_exchange(send2, recv2, 1, b)

    low = lax.rem(lax.broadcasted_iota(jnp.int32, (2 * ML, 128), 1), 64) < KM
    for b in range(2):
        finish(recv2, 1, b, NC)
        ins = recv2[b].astype(F32)
        for half in range(NC):
            outs = []
            for o in (2 * half, 2 * half + 1):
                re = jnp.zeros((ML, 128), F32)
                im = jnp.zeros((ML, 128), F32)
                for i in range(NC):
                    s_re, s_im = ins[i, :ML], ins[i, ML:]
                    w_re, w_im = wgt[i, o, 0], wgt[i, o, 1]
                    re = re + (s_re * w_re - s_im * w_im)
                    im = im + (s_re * w_im + s_im * w_re)
                both = jnp.concatenate([re, im], 0)
                outs.append(both + pltpu.roll(both, 128 - KM if o % 2 == 0 else KM, 1))
            send3[b, half] = jnp.where(low, outs[0], outs[1]).astype(BF)
        chan_exchange(send3, recv3, 2, b)

    for b in range(2):
        finish(recv3, 2, b, NC)
        back = jnp.dot(ixb[...], recv3[b].reshape(128, 128), preferred_element_type=F32)
        send4[b] = back.astype(BF).reshape(NS, 16, 128)
        slab_exchange(send4, recv4, 3, b)

    bias[...] = sbuf[...].astype(F32)
    finish(recv4, 3, 0, NS)
    tmp[...] = recv4[0].reshape(512, 128).astype(F32)

    def sent(o, x):
        return pltpu.make_async_copy(obuf.at[o, :, x], done0.at[o, :, x], out_sem.at[o, x])

    inverse(tmp, lhs, iyb, izb, bias[...], obuf, sent)
    finish(recv4, 3, 1, NS)
    back1[...] = recv4[1]
    for b in range(2):
        finish_send(send1, 0, b, NS)
        finish_send(send2, 1, b, NC)
        finish_send(send3, 2, b, NC)
        finish_send(send4, 3, b, NS)
    for o in range(2):
        for x in range(2):
            sent(o, x).wait()


def inverse_kernel(bias, done0, back1, iy, iz, out, tmp, lhs, obuf, sem, out_sem):
    half = pltpu.make_async_copy(done0, out.at[0], sem)
    half.start()
    tmp[...] = back1[...].reshape(512, 128).astype(F32)

    def sent(o, x):
        return pltpu.make_async_copy(obuf.at[o, :, x], out.at[1, o, :, x], out_sem.at[o, x])

    inverse(tmp, lhs, iy, iz, bias[...], obuf, sent)
    for o in range(2):
        for x in range(2):
            sent(o, x).wait()
    half.wait()


def on_device(state_field, spectral_weights, channel_shift):
    wz, wy, wx, ix, iy, iz, ew = make_tables()
    w2d = spectral_weights.transpose(0, 1, 2, 4, 5, 3).reshape(16 * 16 * ML * 4, KM)
    shift = channel_shift.reshape(1, 2)
    anywhere = pl.BlockSpec(memory_space=pltpu.HBM)
    vmem = pl.BlockSpec(memory_space=pltpu.VMEM)
    slots, few = (2, NS, 16, 128), (2, NC, 16, 128)
    planes, pairs = (2, XL, NG, NG), (2, XL // 2, 2, NG, NG)
    operands = (state_field, w2d, wz, wy, wx, ix, ew, iy, iz, shift)
    done0, back1, bias = pl.pallas_call(
        forward_kernel,
        out_shape=(
            jax.ShapeDtypeStruct(pairs, BF),
            jax.ShapeDtypeStruct(slots[1:], BF),
            jax.ShapeDtypeStruct((1, 2), F32),
        ),
        in_specs=[anywhere] * len(operands),
        out_specs=(anywhere, vmem, vmem),
        scratch_shapes=[
            pltpu.VMEM((1, 2), BF),
            pltpu.VMEM((2, *planes), BF),
            *[pltpu.VMEM(t.shape, BF) for t in (w2d, wz, wy, wx, ix, ew, iy, iz)],
            pltpu.VMEM((512, 128), F32),
            pltpu.VMEM((2, 512, 128), F32),
            pltpu.VMEM((NC, 16, 2, ML, 128), F32),
            *[pltpu.VMEM(s, BF) for s in (slots, slots, few, few, few, few, slots, slots)],
            pltpu.VMEM((4 * NG, 256), BF),
            pltpu.VMEM(pairs, BF),
            pltpu.SemaphoreType.DMA((2, 2, 2)),
            pltpu.SemaphoreType.DMA((9,)),
            pltpu.SemaphoreType.DMA((2, 2)),
            pltpu.SemaphoreType.DMA((4, 2)),
            pltpu.SemaphoreType.DMA((4, 2)),
        ],
        compiler_params=pltpu.CompilerParams(
            collective_id=0, has_side_effects=True, vmem_limit_bytes=40 * 2**20
        ),
    )(*[pltpu.with_memory_space_constraint(v, pltpu.HBM) for v in operands])
    return pl.pallas_call(
        inverse_kernel,
        out_shape=jax.ShapeDtypeStruct((2, *pairs), BF),
        in_specs=[vmem, anywhere, vmem, vmem, vmem],
        out_specs=anywhere,
        scratch_shapes=[
            pltpu.VMEM((512, 128), F32),
            pltpu.VMEM((4 * NG, 256), BF),
            pltpu.VMEM(pairs, BF),
            pltpu.SemaphoreType.DMA,
            pltpu.SemaphoreType.DMA((2, 2)),
        ],
        compiler_params=pltpu.CompilerParams(vmem_limit_bytes=40 * 2**20),
    )(bias, done0, back1, iy, iz).reshape(2, *planes)


def solution(mesh):
    return jax.shard_map(
        on_device,
        mesh=mesh,
        in_specs=(
            P(None, "chan", "slab", None, None),
            P(None, None, "chan", None, None, "slab"),
            P("chan"),
        ),
        out_specs=P(None, "chan", "slab", None, None),
        check_vma=False,
    )
```

```python
import jax
import jax.numpy as jnp
import ml_dtypes
import numpy as np
from jax import lax
from jax.experimental import pallas as pl
from jax.experimental.pallas import tpu as pltpu
from jax.sharding import PartitionSpec as P

NG = 256
KM = 32
NS = 32
NC = 8
XL = NG // NS
ML = 2 * KM // NC
F32 = jnp.float32
BF = jnp.bfloat16
MESH = pl.DeviceIdType.MESH
STEPS = sorted(
    ((dy, dz) for dy in range(-1, 3) for dz in range(-3, 5) if (dy, dz) != (0, 0)),
    key=lambda t: (-abs(t[0]), -abs(t[1]), t[1], t[0]),
)


def make_tables():
    j = np.arange(NG)
    f2 = np.arange(2 * KM)
    f2 = np.where(f2 < KM, f2, f2 + NG - 2 * KM)
    unit = np.float32(2.0 * np.pi / NG)
    tz = ((np.arange(KM)[:, None] * j[None, :]) % NG).astype(np.float32) * unit
    t2 = ((f2[:, None] * j[None, :]) % NG).astype(np.float32) * unit
    cz, sz = np.cos(tz), np.sin(tz)
    c2, s2 = np.cos(t2), np.sin(t2)
    fwd, inv = 1.0 / 16.0, 1.0 / 8.0

    wz = np.zeros((2, 2, NG, 2, 2, 2, KM), np.float32)
    for x in range(2):
        for c in range(2):
            wz[x, c, :, 0, x, c, :] = cz.T * fwd
            wz[x, c, :, 1, x, c, :] = -sz.T * fwd
    wz = wz.reshape(4 * NG, 256)
    order = np.concatenate([np.arange(0, 2 * KM, 2), np.arange(1, 2 * KM, 2)])
    wy = np.concatenate([c2[order], s2[order]], 0) * fwd
    c8, s8 = c2.reshape(NC, ML, NG), s2.reshape(NC, ML, NG)
    wx = np.zeros((NC, 2, ML, NG, 2), np.float32)
    wx[:, 0, :, :, 0], wx[:, 0, :, :, 1] = c8, s8
    wx[:, 1, :, :, 0], wx[:, 1, :, :, 1] = -s8, c8
    wx = wx.reshape(2 * 2 * KM, 2 * NG) * fwd
    ix = np.zeros((NG, 2, NC, 2, ML), np.float32)
    ct, st = c8.transpose(2, 0, 1), s8.transpose(2, 0, 1)
    ix[:, 0, :, 0], ix[:, 0, :, 1] = ct, -st
    ix[:, 1, :, 0], ix[:, 1, :, 1] = st, ct
    ix = ix.reshape(2 * NG, 2 * 2 * KM) * inv
    iy = np.zeros((2, NG, 2, 2, KM), np.float32)
    for h in range(2):
        ch, sh = c2[h::2].T, s2[h::2].T
        iy[0, :, h, 0], iy[0, :, h, 1] = ch, -sh
        iy[1, :, h, 0], iy[1, :, h, 1] = sh, ch
    iy = iy.reshape(2 * NG, 4 * KM) * inv
    wk = np.where(np.arange(KM) == 0, 1.0, 2.0)[:, None]
    iz = np.zeros((2, 2, 2, 2, 2, KM, NG), np.float32)
    for x in range(2):
        for o in range(2):
            iz[x, o, 0, x, o] = wk * cz * inv
            iz[x, o, 1, x, o] = -wk * sz * inv
    iz = iz.reshape(4, 256, NG)
    ew = np.zeros((2, KM, 2, 2, 2, KM), np.float32)
    for c in range(2):
        for h in range(2):
            ew[c, :, h, h, c, :] = np.eye(KM)
    ew = ew.reshape(2, KM, 256)
    return tuple(np.asarray(t).astype(ml_dtypes.bfloat16) for t in (wz, wy, wx, ix, iy, iz, ew))


def split_halves(first, second):
    return (
        jnp.concatenate([first[:, :64], second[:, :64]], 1),
        jnp.concatenate([first[:, 64:], second[:, 64:]], 1),
    )


def inverse(wide, lhs, iy, iz, shift, obuf, sent):
    cols = []
    for pair in range(XL // 2):
        parts = []
        for p in range(2):
            a = wide[pl.ds(4 * pair + p, NS, stride=16), :]
            b = wide[pl.ds(4 * pair + 2 + p, NS, stride=16), :]
            parts.append(split_halves(a, b))
        cols.append(jnp.concatenate([parts[p][h] for h in range(2) for p in range(2)], 0))
    cols = jnp.concatenate(cols, 1).astype(BF)
    u = jnp.dot(iy[...], cols, preferred_element_type=F32).astype(BF)
    for pair in range(XL // 2):
        for q in range(2):
            lhs[pair * NG : (pair + 1) * NG, q * 128 : (q + 1) * 128] = u[
                q * NG : (q + 1) * NG, pair * 128 : (pair + 1) * 128
            ]
    for x in range(2):
        for o in range(2):
            for h in range(2):
                v = jnp.dot(
                    lhs[2 * h * NG : 2 * (h + 1) * NG, :], iz[2 * x + o], preferred_element_type=F32
                )
                v = v + shift[:, o : o + 1]
                v = (0.5 * v * (1.0 + lax.erf(v * np.float32(np.sqrt(0.5))))).astype(BF)
                for at in range(2):
                    obuf[o, 2 * h + at, x] = v[at * NG : (at + 1) * NG]
            sent(o, x).start()


def forward_kernel(
    state, w2d, wz, wy, wx, ix, ew, iy, iz, shift, done0, back1, bias,
    sbuf, xbuf, wraw, wzb, wyb, wxb, ixb, ewb, iyb, izb, tmp, wtmp, wgt,
    send1, recv1, send2, recv2, send3, recv3, send4, recv4, lhs, obuf,
    in_sem, tab_sem, out_sem, ssem, rsem,
):
    slab = lax.axis_index("slab")
    chan = lax.axis_index("chan")

    tables = ((wz, wzb), (wy, wyb), (w2d, wraw), (wx, wxb), (ix, ixb), (ew, ewb), (iy, iyb), (iz, izb), (shift, sbuf))
    loads = [pltpu.make_async_copy(src, dst, tab_sem.at[at]) for at, (src, dst) in enumerate(tables)]
    planes = [
        [
            pltpu.make_async_copy(
                state.at[b, c, pl.ds(4 * h, 4)], xbuf.at[b, c, pl.ds(4 * h, 4)], in_sem.at[b, h, c]
            )
            for h in range(2)
            for c in range(2)
        ]
        for b in range(2)
    ]
    loads[0].start()
    for copy in planes[0]:
        copy.start()
    loads[1].start()
    for copy in planes[1]:
        copy.start()
    for at in (2, 5, 3, 4, 6, 7, 8):
        loads[at].start()

    barrier = pltpu.get_barrier_semaphore()

    def greet_slab(j, carry):
        pl.semaphore_signal(
            barrier, inc=1, device_id=(lax.rem(slab + j, NS), chan), device_id_type=MESH
        )
        return carry

    def greet_chan(j, carry):
        pl.semaphore_signal(
            barrier, inc=1, device_id=(slab, lax.rem(chan + j, NC)), device_id_type=MESH
        )
        return carry

    lax.fori_loop(1, NS, greet_slab, 0)
    lax.fori_loop(1, NC, greet_chan, 0)

    def slab_exchange(send, recv, at, b):
        for dy, dz in STEPS:
            peer = lax.rem(slab // 8 + dy + 4, 4) * 8 + lax.rem(lax.rem(slab, 8) + dz + 8, 8)
            pltpu.make_async_remote_copy(
                src_ref=send.at[b, peer],
                dst_ref=recv.at[b, slab],
                send_sem=ssem.at[at, b],
                recv_sem=rsem.at[at, b],
                device_id=(peer, chan),
                device_id_type=MESH,
            ).start()
        recv[b, slab] = send[b, slab]

    def chan_exchange(send, recv, at, b):
        for j in (4, 5, 3, 2, 6, 7, 1):
            peer = lax.rem(chan + j, NC)
            pltpu.make_async_remote_copy(
                src_ref=send.at[b, peer],
                dst_ref=recv.at[b, chan],
                send_sem=ssem.at[at, b],
                recv_sem=rsem.at[at, b],
                device_id=(slab, peer),
                device_id_type=MESH,
            ).start()
        recv[b, chan] = send[b, chan]

    def finish(recv, at, b, n):
        some = recv.at[b, pl.ds(0, n - 1)]
        pltpu.make_async_copy(some, some, rsem.at[at, b]).wait()

    def finish_send(send, at, b, n):
        some = send.at[b, pl.ds(0, n - 1)]
        pltpu.make_async_copy(some, some, ssem.at[at, b]).wait()

    loads[0].wait()
    for b in range(2):
        for h in range(2):
            for copy in planes[b][2 * h : 2 * h + 2]:
                copy.wait()
            if b == 0 and h == 0:
                loads[1].wait()
            for pair in (2 * h, 2 * h + 1):
                four = jnp.concatenate(
                    [xbuf[b, c, 2 * pair + x] for x in range(2) for c in range(2)], axis=1
                )
                coef_z = jnp.dot(four, wzb[...], preferred_element_type=F32).astype(BF)
                u = jnp.dot(wyb[...], coef_z, preferred_element_type=F32)
                re = u[:64, :128] + u[64:, 128:]
                im = u[:64, 128:] - u[64:, :128]
                for q, val in enumerate((re, im)):
                    for x, rows in enumerate(split_halves(val[:NS], val[NS:])):
                        tmp[pl.ds(2 * (2 * pair + x) + q, NS, stride=16), :] = rows
        send1[b] = tmp[...].astype(BF).reshape(NS, 16, 128)
        if b == 0:
            pl.semaphore_wait(barrier, NS - 1 + NC - 1)
        slab_exchange(send1, recv1, 0, b)

    loads[2].wait()
    loads[5].wait()

    def lay(i, carry):
        even = wraw[pl.ds(pl.multiple_of(i * 1024, 512), 512), :]
        odd = wraw[pl.ds(pl.multiple_of(i * 1024 + 512, 512), 512), :]
        spread = jnp.dot(even, ewb[0], preferred_element_type=F32) + jnp.dot(
            odd, ewb[1], preferred_element_type=F32
        )
        wtmp[0] = spread[:, :128]
        wtmp[1] = spread[:, 128:]
        for o in range(16):
            for q in range(2):
                wgt[i, o, q] = (
                    wtmp[0, pl.ds(o * 32 + 2 * q, ML, stride=4), :]
                    + wtmp[1, pl.ds(o * 32 + 2 * q + 1, ML, stride=4), :]
                )
        return carry

    lax.fori_loop(0, NC, lay, 0)
    for at in (3, 4, 6, 7, 8):
        loads[at].wait()

    for b in range(2):
        finish(recv1, 0, b, NS)
        spectra = jnp.dot(wxb[...], recv1[b].reshape(512, 128), preferred_element_type=F32)
        send2[b] = spectra.astype(BF).reshape(NC, 16, 128)
        chan_exchange(send2, recv2, 1, b)

    low = lax.rem(lax.broadcasted_iota(jnp.int32, (2 * ML, 128), 1), 64) < KM
    for b in range(2):
        finish(recv2, 1, b, NC)
        ins = recv2[b].astype(F32)
        for half in range(NC):
            outs = []
            for o in (2 * half, 2 * half + 1):
                re = jnp.zeros((ML, 128), F32)
                im = jnp.zeros((ML, 128), F32)
                for i in range(NC):
                    s_re, s_im = ins[i, :ML], ins[i, ML:]
                    w_re, w_im = wgt[i, o, 0], wgt[i, o, 1]
                    re = re + (s_re * w_re - s_im * w_im)
                    im = im + (s_re * w_im + s_im * w_re)
                both = jnp.concatenate([re, im], 0)
                outs.append(both + pltpu.roll(both, 128 - KM if o % 2 == 0 else KM, 1))
            send3[b, half] = jnp.where(low, outs[0], outs[1]).astype(BF)
        chan_exchange(send3, recv3, 2, b)

    for b in range(2):
        finish(recv3, 2, b, NC)
        back = jnp.dot(ixb[...], recv3[b].reshape(128, 128), preferred_element_type=F32)
        send4[b] = back.astype(BF).reshape(NS, 16, 128)
        slab_exchange(send4, recv4, 3, b)

    bias[...] = sbuf[...].astype(F32)
    finish(recv4, 3, 0, NS)
    tmp[...] = recv4[0].reshape(512, 128).astype(F32)

    def sent(o, x):
        return pltpu.make_async_copy(obuf.at[o, :, x], done0.at[o, :, x], out_sem.at[o, x])

    inverse(tmp, lhs, iyb, izb, bias[...], obuf, sent)
    finish(recv4, 3, 1, NS)
    back1[...] = recv4[1]
    for b in range(2):
        finish_send(send1, 0, b, NS)
        finish_send(send2, 1, b, NC)
        finish_send(send3, 2, b, NC)
        finish_send(send4, 3, b, NS)
    for o in range(2):
        for x in range(2):
            sent(o, x).wait()


def inverse_kernel(bias, done0, back1, iy, iz, out, tmp, lhs, obuf, sem, out_sem):
    half = pltpu.make_async_copy(done0, out.at[0], sem)
    half.start()
    tmp[...] = back1[...].reshape(512, 128).astype(F32)

    def sent(o, x):
        return pltpu.make_async_copy(obuf.at[o, :, x], out.at[1, o, :, x], out_sem.at[o, x])

    inverse(tmp, lhs, iy, iz, bias[...], obuf, sent)
    for o in range(2):
        for x in range(2):
            sent(o, x).wait()
    half.wait()


def on_device(state_field, spectral_weights, channel_shift):
    wz, wy, wx, ix, iy, iz, ew = make_tables()
    w2d = spectral_weights.transpose(0, 1, 2, 4, 5, 3).reshape(16 * 16 * ML * 4, KM)
    shift = channel_shift.reshape(1, 2)
    anywhere = pl.BlockSpec(memory_space=pltpu.HBM)
    vmem = pl.BlockSpec(memory_space=pltpu.VMEM)
    slots, few = (2, NS, 16, 128), (2, NC, 16, 128)
    planes, pairs = (2, XL, NG, NG), (2, XL // 2, 2, NG, NG)
    operands = (state_field, w2d, wz, wy, wx, ix, ew, iy, iz, shift)
    done0, back1, bias = pl.pallas_call(
        forward_kernel,
        out_shape=(
            jax.ShapeDtypeStruct(pairs, BF),
            jax.ShapeDtypeStruct(slots[1:], BF),
            jax.ShapeDtypeStruct((1, 2), F32),
        ),
        in_specs=[anywhere] * len(operands),
        out_specs=(anywhere, vmem, vmem),
        scratch_shapes=[
            pltpu.VMEM((1, 2), BF),
            pltpu.VMEM((2, *planes), BF),
            *[pltpu.VMEM(t.shape, BF) for t in (w2d, wz, wy, wx, ix, ew, iy, iz)],
            pltpu.VMEM((512, 128), F32),
            pltpu.VMEM((2, 512, 128), F32),
            pltpu.VMEM((NC, 16, 2, ML, 128), F32),
            *[pltpu.VMEM(s, BF) for s in (slots, slots, few, few, few, few, slots, slots)],
            pltpu.VMEM((4 * NG, 256), BF),
            pltpu.VMEM(pairs, BF),
            pltpu.SemaphoreType.DMA((2, 2, 2)),
            pltpu.SemaphoreType.DMA((9,)),
            pltpu.SemaphoreType.DMA((2, 2)),
            pltpu.SemaphoreType.DMA((4, 2)),
            pltpu.SemaphoreType.DMA((4, 2)),
        ],
        compiler_params=pltpu.CompilerParams(
            collective_id=0, has_side_effects=True, vmem_limit_bytes=40 * 2**20
        ),
    )(*[pltpu.with_memory_space_constraint(v, pltpu.HBM) for v in operands])
    return pl.pallas_call(
        inverse_kernel,
        out_shape=jax.ShapeDtypeStruct((2, *pairs), BF),
        in_specs=[vmem, anywhere, vmem, vmem, vmem],
        out_specs=anywhere,
        scratch_shapes=[
            pltpu.VMEM((512, 128), F32),
            pltpu.VMEM((4 * NG, 256), BF),
            pltpu.VMEM(pairs, BF),
            pltpu.SemaphoreType.DMA,
            pltpu.SemaphoreType.DMA((2, 2)),
        ],
        compiler_params=pltpu.CompilerParams(vmem_limit_bytes=40 * 2**20),
    )(bias, done0, back1, iy, iz).reshape(2, *planes)


def solution(mesh):
    return jax.shard_map(
        on_device,
        mesh=mesh,
        in_specs=(
            P(None, "chan", "slab", None, None),
            P(None, None, "chan", None, None, "slab"),
            P("chan"),
        ),
        out_specs=P(None, "chan", "slab", None, None),
        check_vma=False,
    )
```

```python
import jax
import jax.numpy as jnp
import ml_dtypes
import numpy as np
from jax import lax
from jax.experimental import pallas as pl
from jax.experimental.pallas import tpu as pltpu
from jax.sharding import PartitionSpec as P

NG = 256
KM = 32
NS = 32
NC = 8
XL = NG // NS
ML = 2 * KM // NC
F32 = jnp.float32
BF = jnp.bfloat16
MESH = pl.DeviceIdType.MESH
STEPS = sorted(
    ((dy, dz) for dy in range(-1, 3) for dz in range(-3, 5) if (dy, dz) != (0, 0)),
    key=lambda t: (-abs(t[0]), -abs(t[1]), t[1], t[0]),
)


def make_tables():
    j = np.arange(NG)
    f2 = np.arange(2 * KM)
    f2 = np.where(f2 < KM, f2, f2 + NG - 2 * KM)
    unit = np.float32(2.0 * np.pi / NG)
    tz = ((np.arange(KM)[:, None] * j[None, :]) % NG).astype(np.float32) * unit
    t2 = ((f2[:, None] * j[None, :]) % NG).astype(np.float32) * unit
    cz, sz = np.cos(tz), np.sin(tz)
    c2, s2 = np.cos(t2), np.sin(t2)
    fwd, inv = 1.0 / 16.0, 1.0 / 8.0

    wz = np.zeros((2, 2, NG, 2, 2, 2, KM), np.float32)
    for x in range(2):
        for c in range(2):
            wz[x, c, :, 0, x, c, :] = cz.T * fwd
            wz[x, c, :, 1, x, c, :] = -sz.T * fwd
    wz = wz.reshape(4 * NG, 256)
    order = np.concatenate([np.arange(0, 2 * KM, 2), np.arange(1, 2 * KM, 2)])
    wy = np.concatenate([c2[order], s2[order]], 0) * fwd
    c8, s8 = c2.reshape(NC, ML, NG), s2.reshape(NC, ML, NG)
    wx = np.zeros((NC, 2, ML, NG, 2), np.float32)
    wx[:, 0, :, :, 0], wx[:, 0, :, :, 1] = c8, s8
    wx[:, 1, :, :, 0], wx[:, 1, :, :, 1] = -s8, c8
    wx = wx.reshape(2 * 2 * KM, 2 * NG) * fwd
    ix = np.zeros((NG, 2, NC, 2, ML), np.float32)
    ct, st = c8.transpose(2, 0, 1), s8.transpose(2, 0, 1)
    ix[:, 0, :, 0], ix[:, 0, :, 1] = ct, -st
    ix[:, 1, :, 0], ix[:, 1, :, 1] = st, ct
    ix = ix.reshape(2 * NG, 2 * 2 * KM) * inv
    iy = np.zeros((2, NG, 2, 2, KM), np.float32)
    for h in range(2):
        ch, sh = c2[h::2].T, s2[h::2].T
        iy[0, :, h, 0], iy[0, :, h, 1] = ch, -sh
        iy[1, :, h, 0], iy[1, :, h, 1] = sh, ch
    iy = iy.reshape(2 * NG, 4 * KM) * inv
    wk = np.where(np.arange(KM) == 0, 1.0, 2.0)[:, None]
    iz = np.zeros((2, 2, 2, 2, 2, KM, NG), np.float32)
    for x in range(2):
        for o in range(2):
            iz[x, o, 0, x, o] = wk * cz * inv
            iz[x, o, 1, x, o] = -wk * sz * inv
    iz = iz.reshape(4, 256, NG)
    ew = np.zeros((2, KM, 2, 2, 2, KM), np.float32)
    for c in range(2):
        for h in range(2):
            ew[c, :, h, h, c, :] = np.eye(KM)
    ew = ew.reshape(2, KM, 256)
    return tuple(np.asarray(t).astype(ml_dtypes.bfloat16) for t in (wz, wy, wx, ix, iy, iz, ew))


def split_halves(first, second):
    return (
        jnp.concatenate([first[:, :64], second[:, :64]], 1),
        jnp.concatenate([first[:, 64:], second[:, 64:]], 1),
    )


def inverse(wide, lhs, iy, iz, shift, obuf, sent):
    cols = []
    for pair in range(XL // 2):
        parts = []
        for p in range(2):
            a = wide[pl.ds(4 * pair + p, NS, stride=16), :]
            b = wide[pl.ds(4 * pair + 2 + p, NS, stride=16), :]
            parts.append(split_halves(a, b))
        cols.append(jnp.concatenate([parts[p][h] for h in range(2) for p in range(2)], 0))
    cols = jnp.concatenate(cols, 1).astype(BF)
    u = jnp.dot(iy[...], cols, preferred_element_type=F32).astype(BF)
    for pair in range(XL // 2):
        for q in range(2):
            lhs[pair * NG : (pair + 1) * NG, q * 128 : (q + 1) * 128] = u[
                q * NG : (q + 1) * NG, pair * 128 : (pair + 1) * 128
            ]
    for x in range(2):
        for o in range(2):
            for h in range(2):
                v = jnp.dot(
                    lhs[2 * h * NG : 2 * (h + 1) * NG, :], iz[2 * x + o], preferred_element_type=F32
                )
                v = v + shift[:, o : o + 1]
                v = (0.5 * v * (1.0 + lax.erf(v * np.float32(np.sqrt(0.5))))).astype(BF)
                for at in range(2):
                    obuf[o, 2 * h + at, x] = v[at * NG : (at + 1) * NG]
            sent(o, x).start()


def forward_kernel(
    state, w2d, wz, wy, wx, ix, ew, iy, iz, shift, done0, back1, bias,
    sbuf, xbuf, wraw, wzb, wyb, wxb, ixb, ewb, iyb, izb, tmp, wtmp, wgt,
    send1, recv1, send2, recv2, send3, recv3, send4, recv4, lhs, obuf,
    in_sem, tab_sem, out_sem, ssem, rsem,
):
    slab = lax.axis_index("slab")
    chan = lax.axis_index("chan")

    tables = ((wz, wzb), (wy, wyb), (w2d, wraw), (wx, wxb), (ix, ixb), (ew, ewb), (iy, iyb), (iz, izb), (shift, sbuf))
    loads = [pltpu.make_async_copy(src, dst, tab_sem.at[at]) for at, (src, dst) in enumerate(tables)]
    planes = [
        [
            pltpu.make_async_copy(
                state.at[b, c, pl.ds(4 * h, 4)], xbuf.at[b, c, pl.ds(4 * h, 4)], in_sem.at[b, h, c]
            )
            for h in range(2)
            for c in range(2)
        ]
        for b in range(2)
    ]
    loads[0].start()
    for copy in planes[0]:
        copy.start()
    loads[1].start()
    for copy in planes[1]:
        copy.start()
    for at in (2, 5, 3, 4, 6, 7, 8):
        loads[at].start()

    barrier = pltpu.get_barrier_semaphore()

    def greet_slab(j, carry):
        pl.semaphore_signal(
            barrier, inc=1, device_id=(lax.rem(slab + j, NS), chan), device_id_type=MESH
        )
        return carry

    def greet_chan(j, carry):
        pl.semaphore_signal(
            barrier, inc=1, device_id=(slab, lax.rem(chan + j, NC)), device_id_type=MESH
        )
        return carry

    lax.fori_loop(1, NS, greet_slab, 0)
    lax.fori_loop(1, NC, greet_chan, 0)

    def slab_exchange(send, recv, at, b):
        for dy, dz in STEPS:
            peer = lax.rem(slab // 8 + dy + 4, 4) * 8 + lax.rem(lax.rem(slab, 8) + dz + 8, 8)
            pltpu.make_async_remote_copy(
                src_ref=send.at[b, peer],
                dst_ref=recv.at[b, slab],
                send_sem=ssem.at[at, b],
                recv_sem=rsem.at[at, b],
                device_id=(peer, chan),
                device_id_type=MESH,
            ).start()
        recv[b, slab] = send[b, slab]

    def chan_exchange(send, recv, at, b):
        for dx, dc in ((2, 1), (2, 0), (1, 1), (3, 1), (1, 0), (3, 0), (0, 1)):
            peer = lax.rem(chan // 2 + dx, 4) * 2 + lax.rem(chan + dc, 2)
            pltpu.make_async_remote_copy(
                src_ref=send.at[b, peer],
                dst_ref=recv.at[b, chan],
                send_sem=ssem.at[at, b],
                recv_sem=rsem.at[at, b],
                device_id=(slab, peer),
                device_id_type=MESH,
            ).start()
        recv[b, chan] = send[b, chan]

    def finish(recv, at, b, n):
        some = recv.at[b, pl.ds(0, n - 1)]
        pltpu.make_async_copy(some, some, rsem.at[at, b]).wait()

    def finish_send(send, at, b, n):
        some = send.at[b, pl.ds(0, n - 1)]
        pltpu.make_async_copy(some, some, ssem.at[at, b]).wait()

    loads[0].wait()
    for b in range(2):
        for h in range(2):
            for copy in planes[b][2 * h : 2 * h + 2]:
                copy.wait()
            if b == 0 and h == 0:
                loads[1].wait()
            for pair in (2 * h, 2 * h + 1):
                four = jnp.concatenate(
                    [xbuf[b, c, 2 * pair + x] for x in range(2) for c in range(2)], axis=1
                )
                coef_z = jnp.dot(four, wzb[...], preferred_element_type=F32).astype(BF)
                u = jnp.dot(wyb[...], coef_z, preferred_element_type=F32)
                re = u[:64, :128] + u[64:, 128:]
                im = u[:64, 128:] - u[64:, :128]
                for q, val in enumerate((re, im)):
                    for x, rows in enumerate(split_halves(val[:NS], val[NS:])):
                        tmp[pl.ds(2 * (2 * pair + x) + q, NS, stride=16), :] = rows
        send1[b] = tmp[...].astype(BF).reshape(NS, 16, 128)
        if b == 0:
            pl.semaphore_wait(barrier, NS - 1 + NC - 1)
        slab_exchange(send1, recv1, 0, b)

    loads[2].wait()
    loads[5].wait()

    def lay(i, carry):
        even = wraw[pl.ds(pl.multiple_of(i * 1024, 512), 512), :]
        odd = wraw[pl.ds(pl.multiple_of(i * 1024 + 512, 512), 512), :]
        spread = jnp.dot(even, ewb[0], preferred_element_type=F32) + jnp.dot(
            odd, ewb[1], preferred_element_type=F32
        )
        wtmp[0] = spread[:, :128]
        wtmp[1] = spread[:, 128:]
        for o in range(16):
            for q in range(2):
                wgt[i, o, q] = (
                    wtmp[0, pl.ds(o * 32 + 2 * q, ML, stride=4), :]
                    + wtmp[1, pl.ds(o * 32 + 2 * q + 1, ML, stride=4), :]
                )
        return carry

    lax.fori_loop(0, NC, lay, 0)
    for at in (3, 4, 6, 7, 8):
        loads[at].wait()

    for b in range(2):
        finish(recv1, 0, b, NS)
        spectra = jnp.dot(wxb[...], recv1[b].reshape(512, 128), preferred_element_type=F32)
        send2[b] = spectra.astype(BF).reshape(NC, 16, 128)
        chan_exchange(send2, recv2, 1, b)

    low = lax.rem(lax.broadcasted_iota(jnp.int32, (2 * ML, 128), 1), 64) < KM
    for b in range(2):
        finish(recv2, 1, b, NC)
        ins = recv2[b].astype(F32)
        for half in range(NC):
            outs = []
            for o in (2 * half, 2 * half + 1):
                re = jnp.zeros((ML, 128), F32)
                im = jnp.zeros((ML, 128), F32)
                for i in range(NC):
                    s_re, s_im = ins[i, :ML], ins[i, ML:]
                    w_re, w_im = wgt[i, o, 0], wgt[i, o, 1]
                    re = re + (s_re * w_re - s_im * w_im)
                    im = im + (s_re * w_im + s_im * w_re)
                both = jnp.concatenate([re, im], 0)
                outs.append(both + pltpu.roll(both, 128 - KM if o % 2 == 0 else KM, 1))
            send3[b, half] = jnp.where(low, outs[0], outs[1]).astype(BF)
        chan_exchange(send3, recv3, 2, b)

    for b in range(2):
        finish(recv3, 2, b, NC)
        back = jnp.dot(ixb[...], recv3[b].reshape(128, 128), preferred_element_type=F32)
        send4[b] = back.astype(BF).reshape(NS, 16, 128)
        slab_exchange(send4, recv4, 3, b)

    bias[...] = sbuf[...].astype(F32)
    finish(recv4, 3, 0, NS)
    tmp[...] = recv4[0].reshape(512, 128).astype(F32)

    def sent(o, x):
        return pltpu.make_async_copy(obuf.at[o, :, x], done0.at[o, :, x], out_sem.at[o, x])

    inverse(tmp, lhs, iyb, izb, bias[...], obuf, sent)
    finish(recv4, 3, 1, NS)
    back1[...] = recv4[1]
    for b in range(2):
        finish_send(send1, 0, b, NS)
        finish_send(send2, 1, b, NC)
        finish_send(send3, 2, b, NC)
        finish_send(send4, 3, b, NS)
    for o in range(2):
        for x in range(2):
            sent(o, x).wait()


def inverse_kernel(bias, done0, back1, iy, iz, out, tmp, lhs, obuf, sem, out_sem):
    half = pltpu.make_async_copy(done0, out.at[0], sem)
    half.start()
    tmp[...] = back1[...].reshape(512, 128).astype(F32)

    def sent(o, x):
        return pltpu.make_async_copy(obuf.at[o, :, x], out.at[1, o, :, x], out_sem.at[o, x])

    inverse(tmp, lhs, iy, iz, bias[...], obuf, sent)
    for o in range(2):
        for x in range(2):
            sent(o, x).wait()
    half.wait()


def on_device(state_field, spectral_weights, channel_shift):
    wz, wy, wx, ix, iy, iz, ew = make_tables()
    w2d = spectral_weights.transpose(0, 1, 2, 4, 5, 3).reshape(16 * 16 * ML * 4, KM)
    shift = channel_shift.reshape(1, 2)
    anywhere = pl.BlockSpec(memory_space=pltpu.HBM)
    vmem = pl.BlockSpec(memory_space=pltpu.VMEM)
    slots, few = (2, NS, 16, 128), (2, NC, 16, 128)
    planes, pairs = (2, XL, NG, NG), (2, XL // 2, 2, NG, NG)
    operands = (state_field, w2d, wz, wy, wx, ix, ew, iy, iz, shift)
    done0, back1, bias = pl.pallas_call(
        forward_kernel,
        out_shape=(
            jax.ShapeDtypeStruct(pairs, BF),
            jax.ShapeDtypeStruct(slots[1:], BF),
            jax.ShapeDtypeStruct((1, 2), F32),
        ),
        in_specs=[anywhere] * len(operands),
        out_specs=(anywhere, vmem, vmem),
        scratch_shapes=[
            pltpu.VMEM((1, 2), BF),
            pltpu.VMEM((2, *planes), BF),
            *[pltpu.VMEM(t.shape, BF) for t in (w2d, wz, wy, wx, ix, ew, iy, iz)],
            pltpu.VMEM((512, 128), F32),
            pltpu.VMEM((2, 512, 128), F32),
            pltpu.VMEM((NC, 16, 2, ML, 128), F32),
            *[pltpu.VMEM(s, BF) for s in (slots, slots, few, few, few, few, slots, slots)],
            pltpu.VMEM((4 * NG, 256), BF),
            pltpu.VMEM(pairs, BF),
            pltpu.SemaphoreType.DMA((2, 2, 2)),
            pltpu.SemaphoreType.DMA((9,)),
            pltpu.SemaphoreType.DMA((2, 2)),
            pltpu.SemaphoreType.DMA((4, 2)),
            pltpu.SemaphoreType.DMA((4, 2)),
        ],
        compiler_params=pltpu.CompilerParams(
            collective_id=0, has_side_effects=True, vmem_limit_bytes=40 * 2**20
        ),
    )(*[pltpu.with_memory_space_constraint(v, pltpu.HBM) for v in operands])
    return pl.pallas_call(
        inverse_kernel,
        out_shape=jax.ShapeDtypeStruct((2, *pairs), BF),
        in_specs=[vmem, anywhere, vmem, vmem, vmem],
        out_specs=anywhere,
        scratch_shapes=[
            pltpu.VMEM((512, 128), F32),
            pltpu.VMEM((4 * NG, 256), BF),
            pltpu.VMEM(pairs, BF),
            pltpu.SemaphoreType.DMA,
            pltpu.SemaphoreType.DMA((2, 2)),
        ],
        compiler_params=pltpu.CompilerParams(vmem_limit_bytes=40 * 2**20),
    )(bias, done0, back1, iy, iz).reshape(2, *planes)


def solution(mesh):
    return jax.shard_map(
        on_device,
        mesh=mesh,
        in_specs=(
            P(None, "chan", "slab", None, None),
            P(None, None, "chan", None, None, "slab"),
            P("chan"),
        ),
        out_specs=P(None, "chan", "slab", None, None),
        check_vma=False,
    )
```

```python
import jax
import jax.numpy as jnp
import ml_dtypes
import numpy as np
from jax import lax
from jax.experimental import pallas as pl
from jax.experimental.pallas import tpu as pltpu
from jax.sharding import PartitionSpec as P

NG = 256
KM = 32
NS = 32
NC = 8
XL = NG // NS
ML = 2 * KM // NC
F32 = jnp.float32
BF = jnp.bfloat16
MESH = pl.DeviceIdType.MESH
STEPS = sorted(
    ((dy, dz) for dy in range(-1, 3) for dz in range(-3, 5) if (dy, dz) != (0, 0)),
    key=lambda t: (-abs(t[0]), -abs(t[1]), t[1], t[0]),
)


def make_tables():
    j = np.arange(NG)
    f2 = np.arange(2 * KM)
    f2 = np.where(f2 < KM, f2, f2 + NG - 2 * KM)
    unit = np.float32(2.0 * np.pi / NG)
    tz = ((np.arange(KM)[:, None] * j[None, :]) % NG).astype(np.float32) * unit
    t2 = ((f2[:, None] * j[None, :]) % NG).astype(np.float32) * unit
    cz, sz = np.cos(tz), np.sin(tz)
    c2, s2 = np.cos(t2), np.sin(t2)
    fwd, inv = 1.0 / 16.0, 1.0 / 8.0

    wz = np.zeros((2, 2, NG, 2, 2, 2, KM), np.float32)
    for x in range(2):
        for c in range(2):
            wz[x, c, :, 0, x, c, :] = cz.T * fwd
            wz[x, c, :, 1, x, c, :] = -sz.T * fwd
    wz = wz.reshape(4 * NG, 256)
    order = np.concatenate([np.arange(0, 2 * KM, 2), np.arange(1, 2 * KM, 2)])
    wy = np.concatenate([c2[order], s2[order]], 0) * fwd
    c8, s8 = c2.reshape(NC, ML, NG), s2.reshape(NC, ML, NG)
    wx = np.zeros((NC, 2, ML, NG, 2), np.float32)
    wx[:, 0, :, :, 0], wx[:, 0, :, :, 1] = c8, s8
    wx[:, 1, :, :, 0], wx[:, 1, :, :, 1] = -s8, c8
    wx = wx.reshape(2 * 2 * KM, 2 * NG) * fwd
    ix = np.zeros((NG, 2, NC, 2, ML), np.float32)
    ct, st = c8.transpose(2, 0, 1), s8.transpose(2, 0, 1)
    ix[:, 0, :, 0], ix[:, 0, :, 1] = ct, -st
    ix[:, 1, :, 0], ix[:, 1, :, 1] = st, ct
    ix = ix.reshape(2 * NG, 2 * 2 * KM) * inv
    iy = np.zeros((2, NG, 2, 2, KM), np.float32)
    for h in range(2):
        ch, sh = c2[h::2].T, s2[h::2].T
        iy[0, :, h, 0], iy[0, :, h, 1] = ch, -sh
        iy[1, :, h, 0], iy[1, :, h, 1] = sh, ch
    iy = iy.reshape(2 * NG, 4 * KM) * inv
    wk = np.where(np.arange(KM) == 0, 1.0, 2.0)[:, None]
    iz = np.zeros((2, 2, 2, 2, 2, KM, NG), np.float32)
    for x in range(2):
        for o in range(2):
            iz[x, o, 0, x, o] = wk * cz * inv
            iz[x, o, 1, x, o] = -wk * sz * inv
    iz = iz.reshape(4, 256, NG)
    ew = np.zeros((2, KM, 2, 2, 2, KM), np.float32)
    for c in range(2):
        for h in range(2):
            ew[c, :, h, h, c, :] = np.eye(KM)
    ew = ew.reshape(2, KM, 256)
    return tuple(np.asarray(t).astype(ml_dtypes.bfloat16) for t in (wz, wy, wx, ix, iy, iz, ew))


def split_halves(first, second):
    return (
        jnp.concatenate([first[:, :64], second[:, :64]], 1),
        jnp.concatenate([first[:, 64:], second[:, 64:]], 1),
    )


def inverse(wide, lhs, iy, iz, shift, obuf, sent):
    cols = []
    for pair in range(XL // 2):
        parts = []
        for p in range(2):
            a = wide[pl.ds(4 * pair + p, NS, stride=16), :]
            b = wide[pl.ds(4 * pair + 2 + p, NS, stride=16), :]
            parts.append(split_halves(a, b))
        cols.append(jnp.concatenate([parts[p][h] for h in range(2) for p in range(2)], 0))
    cols = jnp.concatenate(cols, 1).astype(BF)
    u = jnp.dot(iy[...], cols, preferred_element_type=F32).astype(BF)
    for pair in range(XL // 2):
        for q in range(2):
            lhs[pair * NG : (pair + 1) * NG, q * 128 : (q + 1) * 128] = u[
                q * NG : (q + 1) * NG, pair * 128 : (pair + 1) * 128
            ]
    for x in range(2):
        for o in range(2):
            for h in range(2):
                v = jnp.dot(
                    lhs[2 * h * NG : 2 * (h + 1) * NG, :], iz[2 * x + o], preferred_element_type=F32
                )
                v = v + shift[:, o : o + 1]
                v = (0.5 * v * (1.0 + lax.erf(v * np.float32(np.sqrt(0.5))))).astype(BF)
                for at in range(2):
                    obuf[o, 2 * h + at, x] = v[at * NG : (at + 1) * NG]
            sent(o, x).start()


def forward_kernel(
    state, w2d, wz, wy, wx, ix, ew, iy, iz, shift, done0, back1, bias,
    sbuf, xbuf, wraw, wzb, wyb, wxb, ixb, ewb, iyb, izb, tmp, wtmp, wgt,
    send1, recv1, send2, recv2, send3, recv3, send4, recv4, lhs, obuf,
    in_sem, tab_sem, out_sem, ssem, rsem,
):
    slab = lax.axis_index("slab")
    chan = lax.axis_index("chan")

    tables = ((wz, wzb), (wy, wyb), (w2d, wraw), (wx, wxb), (ix, ixb), (ew, ewb), (iy, iyb), (iz, izb), (shift, sbuf))
    loads = [pltpu.make_async_copy(src, dst, tab_sem.at[at]) for at, (src, dst) in enumerate(tables)]
    planes = [
        [
            pltpu.make_async_copy(
                state.at[b, c, pl.ds(4 * h, 4)], xbuf.at[b, c, pl.ds(4 * h, 4)], in_sem.at[b, h, c]
            )
            for h in range(2)
            for c in range(2)
        ]
        for b in range(2)
    ]
    loads[0].start()
    for copy in planes[0]:
        copy.start()
    loads[1].start()
    for copy in planes[1]:
        copy.start()
    for at in (2, 5, 3, 4, 6, 7, 8):
        loads[at].start()

    barrier = pltpu.get_barrier_semaphore()

    def greet_slab(j, carry):
        pl.semaphore_signal(
            barrier, inc=1, device_id=(lax.rem(slab + j, NS), chan), device_id_type=MESH
        )
        return carry

    def greet_chan(j, carry):
        pl.semaphore_signal(
            barrier, inc=1, device_id=(slab, lax.rem(chan + j, NC)), device_id_type=MESH
        )
        return carry

    lax.fori_loop(1, NS, greet_slab, 0)
    lax.fori_loop(1, NC, greet_chan, 0)

    def slab_exchange(send, recv, at, b):
        for dy, dz in STEPS:
            peer = lax.rem(slab // 8 + dy + 4, 4) * 8 + lax.rem(lax.rem(slab, 8) + dz + 8, 8)
            pltpu.make_async_remote_copy(
                src_ref=send.at[b, peer],
                dst_ref=recv.at[b, slab],
                send_sem=ssem.at[at, b],
                recv_sem=rsem.at[at, b],
                device_id=(peer, chan),
                device_id_type=MESH,
            ).start()
        recv[b, slab] = send[b, slab]

    chan_peers = [
        lax.rem(chan // 2 + dx, 4) * 2 + lax.rem(chan + dc, 2)
        for dx, dc in ((2, 1), (2, 0), (1, 1), (3, 1), (1, 0), (3, 0), (0, 1))
    ]

    def chan_copy(send, recv, at, b, peer):
        pltpu.make_async_remote_copy(
            src_ref=send.at[b, peer],
            dst_ref=recv.at[b, chan],
            send_sem=ssem.at[at, b],
            recv_sem=rsem.at[at, b],
            device_id=(slab, peer),
            device_id_type=MESH,
        ).start()

    def chan_exchange(send, recv, at, b):
        for peer in chan_peers:
            chan_copy(send, recv, at, b, peer)
        recv[b, chan] = send[b, chan]

    def finish(recv, at, b, n):
        some = recv.at[b, pl.ds(0, n - 1)]
        pltpu.make_async_copy(some, some, rsem.at[at, b]).wait()

    def finish_send(send, at, b, n):
        some = send.at[b, pl.ds(0, n - 1)]
        pltpu.make_async_copy(some, some, ssem.at[at, b]).wait()

    loads[0].wait()
    for b in range(2):
        for h in range(2):
            for copy in planes[b][2 * h : 2 * h + 2]:
                copy.wait()
            if b == 0 and h == 0:
                loads[1].wait()
            for pair in (2 * h, 2 * h + 1):
                four = jnp.concatenate(
                    [xbuf[b, c, 2 * pair + x] for x in range(2) for c in range(2)], axis=1
                )
                coef_z = jnp.dot(four, wzb[...], preferred_element_type=F32).astype(BF)
                u = jnp.dot(wyb[...], coef_z, preferred_element_type=F32)
                re = u[:64, :128] + u[64:, 128:]
                im = u[:64, 128:] - u[64:, :128]
                for q, val in enumerate((re, im)):
                    for x, rows in enumerate(split_halves(val[:NS], val[NS:])):
                        tmp[pl.ds(2 * (2 * pair + x) + q, NS, stride=16), :] = rows
        send1[b] = tmp[...].astype(BF).reshape(NS, 16, 128)
        if b == 0:
            pl.semaphore_wait(barrier, NS - 1 + NC - 1)
        slab_exchange(send1, recv1, 0, b)

    loads[2].wait()
    loads[5].wait()

    def lay(i, carry):
        even = wraw[pl.ds(pl.multiple_of(i * 1024, 512), 512), :]
        odd = wraw[pl.ds(pl.multiple_of(i * 1024 + 512, 512), 512), :]
        spread = jnp.dot(even, ewb[0], preferred_element_type=F32) + jnp.dot(
            odd, ewb[1], preferred_element_type=F32
        )
        wtmp[0] = spread[:, :128]
        wtmp[1] = spread[:, 128:]
        for o in range(16):
            for q in range(2):
                wgt[i, o, q] = (
                    wtmp[0, pl.ds(o * 32 + 2 * q, ML, stride=4), :]
                    + wtmp[1, pl.ds(o * 32 + 2 * q + 1, ML, stride=4), :]
                )
        return carry

    lax.fori_loop(0, NC, lay, 0)
    for at in (3, 4, 6, 7, 8):
        loads[at].wait()

    for b in range(2):
        finish(recv1, 0, b, NS)
        spectra = jnp.dot(wxb[...], recv1[b].reshape(512, 128), preferred_element_type=F32)
        send2[b] = spectra.astype(BF).reshape(NC, 16, 128)
        chan_exchange(send2, recv2, 1, b)

    low = lax.rem(lax.broadcasted_iota(jnp.int32, (2 * ML, 128), 1), 64) < KM
    for b in range(2):
        finish(recv2, 1, b, NC)
        ins = recv2[b].astype(F32)
        for half in [*chan_peers, chan]:
            outs = []
            for parity in range(2):
                o = 2 * half + parity
                re = jnp.zeros((ML, 128), F32)
                im = jnp.zeros((ML, 128), F32)
                for i in range(NC):
                    s_re, s_im = ins[i, :ML], ins[i, ML:]
                    w_re, w_im = wgt[i, o, 0], wgt[i, o, 1]
                    re = re + (s_re * w_re - s_im * w_im)
                    im = im + (s_re * w_im + s_im * w_re)
                both = jnp.concatenate([re, im], 0)
                outs.append(both + pltpu.roll(both, 128 - KM if parity == 0 else KM, 1))
            both = jnp.where(low, outs[0], outs[1]).astype(BF)
            if half is chan:
                recv3[b, chan] = both
            else:
                send3[b, half] = both
                chan_copy(send3, recv3, 2, b, half)

    for b in range(2):
        finish(recv3, 2, b, NC)
        back = jnp.dot(ixb[...], recv3[b].reshape(128, 128), preferred_element_type=F32)
        send4[b] = back.astype(BF).reshape(NS, 16, 128)
        slab_exchange(send4, recv4, 3, b)

    bias[...] = sbuf[...].astype(F32)
    finish(recv4, 3, 0, NS)
    tmp[...] = recv4[0].reshape(512, 128).astype(F32)

    def sent(o, x):
        return pltpu.make_async_copy(obuf.at[o, :, x], done0.at[o, :, x], out_sem.at[o, x])

    inverse(tmp, lhs, iyb, izb, bias[...], obuf, sent)
    finish(recv4, 3, 1, NS)
    back1[...] = recv4[1]
    for b in range(2):
        finish_send(send1, 0, b, NS)
        finish_send(send2, 1, b, NC)
        finish_send(send3, 2, b, NC)
        finish_send(send4, 3, b, NS)
    for o in range(2):
        for x in range(2):
            sent(o, x).wait()


def inverse_kernel(bias, done0, back1, iy, iz, out, tmp, lhs, obuf, sem, out_sem):
    half = pltpu.make_async_copy(done0, out.at[0], sem)
    half.start()
    tmp[...] = back1[...].reshape(512, 128).astype(F32)

    def sent(o, x):
        return pltpu.make_async_copy(obuf.at[o, :, x], out.at[1, o, :, x], out_sem.at[o, x])

    inverse(tmp, lhs, iy, iz, bias[...], obuf, sent)
    for o in range(2):
        for x in range(2):
            sent(o, x).wait()
    half.wait()


def on_device(state_field, spectral_weights, channel_shift):
    wz, wy, wx, ix, iy, iz, ew = make_tables()
    w2d = spectral_weights.transpose(0, 1, 2, 4, 5, 3).reshape(16 * 16 * ML * 4, KM)
    shift = channel_shift.reshape(1, 2)
    anywhere = pl.BlockSpec(memory_space=pltpu.HBM)
    vmem = pl.BlockSpec(memory_space=pltpu.VMEM)
    slots, few = (2, NS, 16, 128), (2, NC, 16, 128)
    planes, pairs = (2, XL, NG, NG), (2, XL // 2, 2, NG, NG)
    operands = (state_field, w2d, wz, wy, wx, ix, ew, iy, iz, shift)
    done0, back1, bias = pl.pallas_call(
        forward_kernel,
        out_shape=(
            jax.ShapeDtypeStruct(pairs, BF),
            jax.ShapeDtypeStruct(slots[1:], BF),
            jax.ShapeDtypeStruct((1, 2), F32),
        ),
        in_specs=[anywhere] * len(operands),
        out_specs=(anywhere, vmem, vmem),
        scratch_shapes=[
            pltpu.VMEM((1, 2), BF),
            pltpu.VMEM((2, *planes), BF),
            *[pltpu.VMEM(t.shape, BF) for t in (w2d, wz, wy, wx, ix, ew, iy, iz)],
            pltpu.VMEM((512, 128), F32),
            pltpu.VMEM((2, 512, 128), F32),
            pltpu.VMEM((NC, 16, 2, ML, 128), F32),
            *[pltpu.VMEM(s, BF) for s in (slots, slots, few, few, few, few, slots, slots)],
            pltpu.VMEM((4 * NG, 256), BF),
            pltpu.VMEM(pairs, BF),
            pltpu.SemaphoreType.DMA((2, 2, 2)),
            pltpu.SemaphoreType.DMA((9,)),
            pltpu.SemaphoreType.DMA((2, 2)),
            pltpu.SemaphoreType.DMA((4, 2)),
            pltpu.SemaphoreType.DMA((4, 2)),
        ],
        compiler_params=pltpu.CompilerParams(
            collective_id=0, has_side_effects=True, vmem_limit_bytes=40 * 2**20
        ),
    )(*[pltpu.with_memory_space_constraint(v, pltpu.HBM) for v in operands])
    return pl.pallas_call(
        inverse_kernel,
        out_shape=jax.ShapeDtypeStruct((2, *pairs), BF),
        in_specs=[vmem, anywhere, vmem, vmem, vmem],
        out_specs=anywhere,
        scratch_shapes=[
            pltpu.VMEM((512, 128), F32),
            pltpu.VMEM((4 * NG, 256), BF),
            pltpu.VMEM(pairs, BF),
            pltpu.SemaphoreType.DMA,
            pltpu.SemaphoreType.DMA((2, 2)),
        ],
        compiler_params=pltpu.CompilerParams(vmem_limit_bytes=40 * 2**20),
    )(bias, done0, back1, iy, iz).reshape(2, *planes)


def solution(mesh):
    return jax.shard_map(
        on_device,
        mesh=mesh,
        in_specs=(
            P(None, "chan", "slab", None, None),
            P(None, None, "chan", None, None, "slab"),
            P("chan"),
        ),
        out_specs=P(None, "chan", "slab", None, None),
        check_vma=False,
    )
```
